32 devices in a mesh: grp: 2 (over x), row: 8 (over z, y), col: 2 (over core).
Axes of the slice: x: 2, y: 2, z: 4, core: 2. Of those that a mesh axis runs over, the one named last changes fastest.
Arguments:
- queries: bfloat16 [128, 32, 1024], P(('grp', 'row'), 'col'), parts along dimension 0, may hold values from -4 to 4
- key_map: bfloat16 [128, 32, 1024], P(('grp', 'row'), 'col'), parts along dimension 0, may hold values from -4 to 4
- value_map: bfloat16 [128, 32, 1024], P(('grp', 'row'), 'col'), parts along dimension 0, may hold values from -4 to 4
- saved_output: bfloat16 [128, 32, 1024], P(('grp', 'row'), 'col'), parts along dimension 0, may hold values from -4 to 4, as said below
- output_grad: bfloat16 [128, 32, 1024], P(('grp', 'row'), 'col'), parts along dimension 0, may hold values from -48 to 48
- saved_logsum: float32 [128, 32, 16], P(('grp', 'row'), 'col'), parts along dimension 0, may hold values from -128 to 140, as said below
Outputs:
- query_grad: float32 [128, 32, 1024], P(('grp', 'row'), 'col'), parts along dimension 0
- key_grad: float32 [128, 32, 1024], P(('grp', 'row'), 'col'), parts along dimension 0
- value_grad: float32 [128, 32, 1024], P(('grp', 'row'), 'col'), parts along dimension 0
The draws below stay inside these ranges and needn't reach their ends.
There are 2 independent parts, one for each index of `grp`. The reference program is written for one: setup_inputs(seed, part) draws one part's arguments, and reference() takes and returns one part's arrays. A program takes and returns all parts, laid end to end along the dimension named above; each array names one. Nothing has to cross between parts.
Inputs may be any that keep to these rules, and one draw needn't show every extreme that they name: `saved_output`: the attention output of these queries, keys and values over the stripes of the steps, sum over j of softmax of scores times value_map[j], rounded to bfloat16. `saved_logsum`: for each token and head, the natural logarithm of the sum of exp(scores) over the keys of its stripe.
All inputs are finite; a program needn't handle non-finite values.
Results may differ from the reference program's by a relative error of at most 0.003.
Values may be sent and summed in bfloat16 or wider, within the bound.
A program may use at most 128 MiB of HBM per device.

```python
import math
import jax
import jax.numpy as jnp
from jax import lax

HEADS = 16
HD = 64
SW = 8
HALF = 8
D = 1024
H = 64
W = 32


def row_stripes_drawn(values, last):
    return jnp.moveaxis(values.reshape((H // SW, SW * W) + last), 2, 0)


def column_stripes_drawn(values, last):
    shaped = values.reshape((H, W // SW, SW) + last)
    shaped = jnp.swapaxes(shaped, 0, 1).reshape((W // SW, H * SW) + last)
    return jnp.moveaxis(shaped, 2, 0)


def rows_back_drawn(values):
    return jnp.moveaxis(values, 0, 2).reshape(H, W, -1)


def columns_back_drawn(values):
    shaped = jnp.moveaxis(values, 0, 2).reshape((W // SW, H, SW, -1))
    return jnp.swapaxes(shaped, 0, 1).reshape(H, W, -1)


def base_maps(base_key):
    folded = jax.random.fold_in(base_key, 11)
    first, second, third, fourth = jax.random.split(folded, 4)
    shape = (H, W, HEADS * HD)
    maps = []
    for number, part_key in enumerate((first, second, third)):
        values = jnp.clip(jax.random.normal(part_key, shape, jnp.float32), -4.0, 4.0)
        maps.append(values.astype(jnp.bfloat16))
    return (maps[0], maps[1], maps[2])


def forward_head(pieces):
    query, key_part, value = pieces
    scale = 1.0 / math.sqrt(HD)
    scores = jnp.einsum('gae,gbe->gab', query.astype(jnp.float32), key_part.astype(jnp.float32)) * scale
    top = jnp.max(scores, axis=2, keepdims=True)
    weights = jnp.exp(scores - top)
    total = jnp.sum(weights, axis=2, keepdims=True)
    logsum = top[:, :, 0] + jnp.log(total[:, :, 0])
    output = jnp.einsum('gab,gbe->gae', weights / total, value.astype(jnp.float32))
    return (output, logsum)


def forward_maps(base_key):
    query, key_part, value = base_maps(base_key)
    outputs = []
    sums = []
    for arrange, back, lower, upper in ((row_stripes_drawn, rows_back_drawn, 0, HALF), (column_stripes_drawn, columns_back_drawn, HALF, HEADS)):
        pieces = tuple((arrange(values[:, :, lower * HD:upper * HD], (HALF, HD)) for values in (query, key_part, value)))
        output, logsum = lax.map(forward_head, pieces)
        outputs.append(back(output))
        sums.append(back(logsum))
    saved = jnp.concatenate(outputs, axis=2).astype(jnp.bfloat16)
    return (saved, jnp.concatenate(sums, axis=2).astype(jnp.float32))


def draw_queries(key, part):
    return base_maps(key)[0]


def draw_key_map(key, part):
    return base_maps(key)[1]


def draw_value_map(key, part):
    return base_maps(key)[2]


def draw_saved_output(key, part):
    return forward_maps(key)[0]


def draw_saved_logsum(key, part):
    return forward_maps(key)[1]


def block_levels(stream_key, extent, cuts, least, high):
    gain = 1.0
    for axis_at, parts in cuts:
        heights = jax.random.uniform(jax.random.fold_in(jax.random.fold_in(stream_key, 6), axis_at), (parts,), jnp.float32, least / len(cuts), high / len(cuts))
        gain = gain * jnp.repeat(jnp.exp(heights), extent[axis_at] // parts).reshape((-1,) + (1,) * (len(extent) - 1 - axis_at))
    return gain


def scatter_about(own_key, shape, spread, bound, shards=(), kind=jnp.bfloat16):
    drawn = spread * jax.random.normal(own_key, shape, jnp.float32)
    if shards:
        drawn = drawn * block_levels(own_key, shape, shards, -0.22, 0.18)
    return jnp.clip(drawn, -bound, bound).astype(kind)


def setup_inputs(seed: int = 0, part: int = 0) -> dict:
    seeds = jax.random.split(jax.random.key(seed), 7)
    part_keys = jax.random.split(jax.random.fold_in(seeds[6], part), 7)
    queries = draw_queries(jax.random.fold_in(jax.random.fold_in(seeds[6], part), 71), part)
    key_map = draw_key_map(jax.random.fold_in(jax.random.fold_in(seeds[6], part), 71), part)
    value_map = draw_value_map(jax.random.fold_in(jax.random.fold_in(seeds[6], part), 71), part)
    saved_output = draw_saved_output(jax.random.fold_in(jax.random.fold_in(seeds[6], part), 71), part)
    output_grad = scatter_about(part_keys[4], (H, W, D), 8.0, 48.0, ((0, 8), (1, 2)))
    saved_logsum = draw_saved_logsum(jax.random.fold_in(jax.random.fold_in(seeds[6], part), 71), part)
    return dict(queries=queries, key_map=key_map, value_map=value_map, saved_output=saved_output, output_grad=output_grad, saved_logsum=saved_logsum)


def rounded(values):
    return lax.optimization_barrier(values.astype(jnp.bfloat16)).astype(jnp.float32)

def row_stripes(values, last):
    return jnp.moveaxis(values.reshape((H // SW, SW * W) + last), 2, 0)

def column_stripes(values, last):
    shaped = values.reshape((H, W // SW, SW) + last)
    shaped = jnp.swapaxes(shaped, 0, 1).reshape((W // SW, H * SW) + last)
    return jnp.moveaxis(shaped, 2, 0)

def rows_back(values):
    return jnp.moveaxis(values, 0, 2).reshape(H, W, -1)

def columns_back(values):
    shaped = jnp.moveaxis(values, 0, 2).reshape((W // SW, H, SW, -1))
    return jnp.swapaxes(shaped, 0, 1).reshape(H, W, -1)

def head_grads(pieces):
    query, key_part, value, saved, grad, logsum = pieces
    scale = 1.0 / math.sqrt(HD)
    query_float = query.astype(jnp.float32)
    key_float = key_part.astype(jnp.float32)
    value_float = value.astype(jnp.float32)
    saved_float = saved.astype(jnp.float32)
    grad_float = grad.astype(jnp.float32)
    scores = jnp.einsum('gae,gbe->gab', query_float, key_float) * scale
    probs = jnp.exp(scores - logsum[:, :, None])
    delta = lax.optimization_barrier(jnp.sum(grad_float * saved_float, axis=2))
    grad_probs = jnp.einsum('gae,gbe->gab', grad_float, value_float)
    grad_scores = rounded(probs * (grad_probs - delta[:, :, None]))
    query_grad = jnp.einsum('gab,gbe->gae', grad_scores, key_float) * scale
    key_grad = jnp.einsum('gab,gae->gbe', grad_scores, query_float) * scale
    value_grad = jnp.einsum('gab,gae->gbe', rounded(probs), grad_float)
    return (query_grad, key_grad, value_grad)

def reference(queries, key_map, value_map, saved_output, output_grad, saved_logsum):
    results = []
    for arrange, back, lower, upper in ((row_stripes, rows_back, 0, HALF), (column_stripes, columns_back, HALF, HEADS)):
        pieces = tuple((arrange(values[:, :, lower * HD:upper * HD], (HALF, HD)) for values in (queries, key_map, value_map, saved_output, output_grad)))
        pieces = pieces + (arrange(saved_logsum[:, :, lower:upper], (HALF,)),)
        grads = lax.map(head_grads, pieces)
        results.append(tuple((back(values) for values in grads)))
    query_grad = jnp.concatenate((results[0][0], results[1][0]), axis=2)
    key_grad = jnp.concatenate((results[0][1], results[1][1]), axis=2)
    value_grad = jnp.concatenate((results[0][2], results[1][2]), axis=2)
    return (query_grad, key_grad, value_grad)
```

```python
import functools
import math

import jax
import jax.numpy as jnp
from jax import lax
from jax.experimental import pallas as pl
from jax.experimental.pallas import tpu as pltpu
from jax.sharding import PartitionSpec as P

HEADS = 16
HD = 64
SW = 8


def attention_terms(
    stripe_query, stripe_key, stripe_value, stripe_grad, stripe_logsum, stripe_delta
):
    scale = 1.0 / math.sqrt(HD)
    scores = (
        jnp.einsum("gahe,gbhe->ghab", stripe_query, stripe_key, preferred_element_type=jnp.float32)
        * scale
    )
    probs = jnp.exp(scores - jnp.swapaxes(stripe_logsum, 1, 2)[..., None])
    grad_probs = jnp.einsum(
        "gahe,gbhe->ghab", stripe_grad, stripe_value, preferred_element_type=jnp.float32
    )
    grad_scores = (probs * (grad_probs - jnp.swapaxes(stripe_delta, 1, 2)[..., None])).astype(
        jnp.bfloat16
    )
    return (probs.astype(jnp.bfloat16), grad_scores)


def query_side(grad_scores, stripe_key):
    total = jnp.einsum(
        "ghab,gbhe->gahe", grad_scores, stripe_key, preferred_element_type=jnp.float32
    )
    return total * (1.0 / math.sqrt(HD))


def key_side(probs_half, grad_scores, stripe_query, stripe_grad):
    key_total = jnp.einsum(
        "ghab,gahe->gbhe", grad_scores, stripe_query, preferred_element_type=jnp.float32
    )
    value_total = jnp.einsum(
        "ghab,gahe->gbhe", probs_half, stripe_grad, preferred_element_type=jnp.float32
    )
    return (key_total * (1.0 / math.sqrt(HD)), value_total)


def in_blocks(step, carry, arrays, size):
    length = arrays[0].shape[0]

    def turn(index, total):
        parts = tuple((lax.dynamic_slice_in_dim(array, index * size, size, 0) for array in arrays))
        return step(total, parts)

    return lax.fori_loop(0, length // size, turn, carry)


def local_general(queries, key_map, value_map, saved_output, output_grad, saved_logsum):
    rows, cols, width = queries.shape
    half = HEADS // 2
    split = half * HD
    tail = (half, HD)
    block = 4 * rows
    products = output_grad.astype(jnp.float32) * saved_output.astype(jnp.float32)
    delta_all = jnp.sum(products.reshape(rows, cols, HEADS, HD), axis=3)

    def row_group(values, last):
        return values.reshape((rows // SW, SW * values.shape[1]) + last)

    def column_group(values, last):
        count = values.shape[0]
        shaped = values.reshape((count, cols // SW, SW) + last)
        return jnp.swapaxes(shaped, 0, 1).reshape((cols // SW, count * SW) + last)

    def column_back(values, count):
        shaped = values.reshape((cols // SW, count, SW, -1))
        return jnp.swapaxes(shaped, 0, 1).reshape(count, cols, -1)

    full_key, full_value = (
        lax.all_gather(key_map[:, :, :split], "col", axis=1, tiled=True),
        lax.all_gather(value_map[:, :, :split], "col", axis=1, tiled=True),
    )
    wide = full_key.shape[1]
    stripe_query = row_group(queries[:, :, :split], tail)
    stripe_grad = row_group(output_grad[:, :, :split], tail)
    stripe_logsum = row_group(saved_logsum[:, :, :half], (half,))
    stripe_delta = row_group(delta_all[:, :, :half], (half,))
    stripe_key = row_group(full_key, tail)
    stripe_value = row_group(full_value, tail)
    probs_half, grad_scores = attention_terms(
        stripe_query, stripe_key, stripe_value, stripe_grad, stripe_logsum, stripe_delta
    )
    row_query_grad = query_side(grad_scores, stripe_key).reshape(rows, cols, split)
    row_key_part, row_value_part = key_side(probs_half, grad_scores, stripe_query, stripe_grad)
    row_term = jnp.concatenate(
        (row_key_part.reshape(rows, wide, split), row_value_part.reshape(rows, wide, split)), axis=2
    )
    row_sums = lax.psum_scatter(row_term, "col", scatter_dimension=1, tiled=True)
    local_key = key_map[:, :, split:]
    local_value = value_map[:, :, split:]
    column_query = column_group(queries[:, :, split:], tail)
    column_grad = column_group(output_grad[:, :, split:], tail)
    column_logsum = column_group(saved_logsum[:, :, half:], (half,))
    column_delta = column_group(delta_all[:, :, half:], (half,))

    def query_step(total, pieces):
        grouped_key = column_group(pieces[0], tail)
        grouped_value = column_group(pieces[1], tail)
        weights, gradients = attention_terms(
            column_query, grouped_key, grouped_value, column_grad, column_logsum, column_delta
        )
        return total + query_side(gradients, grouped_key)

    empty_query = jnp.zeros(column_query.shape, jnp.float32)
    every_key, every_value = (
        lax.all_gather(local_key, "row", axis=0, tiled=True),
        lax.all_gather(local_value, "row", axis=0, tiled=True),
    )
    column_total = in_blocks(query_step, empty_query, (every_key, every_value), block)

    def key_step(pieces):
        count = pieces[0].shape[0]
        grouped_key = column_group(pieces[0], tail)
        grouped_value = column_group(pieces[1], tail)
        weights, gradients = attention_terms(
            column_query, grouped_key, grouped_value, column_grad, column_logsum, column_delta
        )
        key_part, value_part = key_side(weights, gradients, column_query, column_grad)
        return jnp.concatenate(
            (column_back(key_part, count), column_back(value_part, count)), axis=2
        )

    count = rows * lax.axis_size("row")
    stacked = lax.map(
        key_step,
        (
            every_key.reshape((count // block, block) + every_key.shape[1:]),
            every_value.reshape((count // block, block) + every_value.shape[1:]),
        ),
    )
    column_sums = lax.psum_scatter(
        stacked.reshape((count,) + stacked.shape[2:]), "row", scatter_dimension=0, tiled=True
    )
    column_key_grad = column_sums[:, :, :split]
    column_value_grad = column_sums[:, :, split:]
    column_query_grad = column_back(column_total, rows)
    query_grad = jnp.concatenate((row_query_grad, column_query_grad), axis=2)
    key_grad = jnp.concatenate((row_sums[:, :, :split], column_key_grad), axis=2)
    value_grad = jnp.concatenate((row_sums[:, :, split:], column_value_grad), axis=2)
    return (query_grad, key_grad, value_grad)


MESH = pl.DeviceIdType.MESH
NT = (((1,), (1,)), ((), ()))
TN = (((0,), (0,)), ((), ()))
PAIR = 2 * HD


def flat(values):
    return values.astype(jnp.float32).reshape((-1, values.shape[-1]))


def attend(count, block, q_s, k_s, v_s, g_s, rows, dq_t, dk_s, dv_s):
    scale = 1.0 / math.sqrt(HD)
    lane = lax.broadcasted_iota(jnp.int32, (block, PAIR), 1)
    masks = tuple(((lane // HD) == h).astype(jnp.float32).astype(jnp.bfloat16) for h in (0, 1))

    def step(j, carry):
        part = pl.ds(pl.multiple_of(j * block, block), block)
        q = q_s[0:count, :]
        g = g_s[0:count, :]
        keys = k_s[part, :]
        values = v_s[part, :]
        dk = []
        dv = []
        dq = None
        for h in (0, 1):
            key = keys * masks[h]
            value = values * masks[h]
            scores = lax.dot_general(key, q, NT, preferred_element_type=jnp.float32)
            probs = jnp.exp(scores * scale - rows[h : h + 1, 0:count])
            grad_probs = lax.dot_general(value, g, NT, preferred_element_type=jnp.float32)
            grad_scores = (probs * (grad_probs - rows[2 + h : 3 + h, 0:count])).astype(jnp.bfloat16)
            half = probs.astype(jnp.bfloat16)
            dv.append(jnp.dot(half, g, preferred_element_type=jnp.float32))
            dk.append(jnp.dot(grad_scores, q, preferred_element_type=jnp.float32))
            term = lax.dot_general(key, grad_scores, TN, preferred_element_type=jnp.float32)
            dq = term if dq is None else dq + term
        dk_s[part, :] = jnp.where(lane < HD, dk[0], dk[1]) * scale
        dv_s[part, :] = jnp.where(lane < HD, dv[0], dv[1])
        dq_t[:, 0:count] += dq
        return carry

    dq_t[:, 0:count] = jnp.zeros((PAIR, count), jnp.float32)
    lax.fori_loop(0, count // block, step, 0)
    return dq_t[:, 0:count].T * scale


def exchange_kernel(
    q_ref, k_ref, v_ref, o_ref, g_ref, l_ref,
    dq_ref, dk_ref, dv_ref,
    col_in, col_aux, row_in, row_aux, aux_row, aux_col, col_out, row_out,
    q_s, k_s, v_s, g_s, rows_s, dq_t, dk_s, dv_s,
    cs_sem, cr_sem, as_sem, ar_sem, rs_sem, rr_sem, os_sem, or_sem, ps_sem, pr_sem,
):
    me = lax.axis_index("row")
    core = lax.axis_index("col")
    peers = lax.axis_size("row")
    other = 1 - core
    split = (HEADS // 2) * HD
    pair = me // 2
    stripe = me % 2
    ins = (q_ref, k_ref, v_ref, g_ref)
    outs = (dq_ref, dk_ref, dv_ref)

    barrier = pltpu.get_barrier_semaphore()
    for step in range(1, peers):
        pl.semaphore_signal(
            barrier, inc=1, device_id={"row": lax.rem(me + step, peers)}, device_id_type=MESH
        )
    pl.semaphore_signal(barrier, inc=1, device_id={"col": other}, device_id_type=MESH)
    pl.semaphore_wait(barrier, peers)

    def col_lanes(index):
        return pl.ds(pl.multiple_of(split + PAIR * index, PAIR), PAIR)

    def core_lanes(index):
        return pl.ds(pl.multiple_of(2 * PAIR * index, 2 * PAIR), 2 * PAIR)

    def eight(index):
        return pl.ds(pl.multiple_of(index * 8, 8), 8)

    def row_copy(a):
        return pltpu.make_async_remote_copy(
            src_ref=ins[a].at[:, :, :, core_lanes(other)],
            dst_ref=row_in.at[a],
            send_sem=rs_sem.at[a], recv_sem=rr_sem.at[a],
            device_id={"col": other}, device_id_type=MESH,
        )

    def col_copy(a, target, source):
        return pltpu.make_async_remote_copy(
            src_ref=ins[a].at[:, target % 2, :, col_lanes(target // 2)],
            dst_ref=col_in.at[a, eight(source)],
            send_sem=cs_sem.at[a, target], recv_sem=cr_sem.at[a, source],
            device_id={"row": target}, device_id_type=MESH,
        )

    def aux_copy(target, source):
        return pltpu.make_async_remote_copy(
            src_ref=aux_col.at[target // 2],
            dst_ref=col_aux.at[source],
            send_sem=as_sem.at[target], recv_sem=ar_sem.at[source],
            device_id={"row": target}, device_id_type=MESH,
        )

    def back_copy(a, target, owner):
        return pltpu.make_async_remote_copy(
            src_ref=col_out.at[a, eight(target)],
            dst_ref=outs[a].at[:, owner % 2, :, col_lanes(owner // 2)],
            send_sem=os_sem.at[a, target], recv_sem=or_sem.at[a, owner],
            device_id={"row": target}, device_id_type=MESH,
        )

    def row_back(a, owner):
        return pltpu.make_async_remote_copy(
            src_ref=row_out.at[a],
            dst_ref=outs[a].at[:, :, :, core_lanes(owner)],
            send_sem=ps_sem.at[a], recv_sem=pr_sem.at[a],
            device_id={"col": other}, device_id_type=MESH,
        )

    def row_aux_copy():
        return pltpu.make_async_remote_copy(
            src_ref=aux_row.at[pl.ds(2 * other, 2)],
            dst_ref=row_aux,
            send_sem=rs_sem.at[4], recv_sem=rr_sem.at[4],
            device_id={"col": other}, device_id_type=MESH,
        )

    for a in range(4):
        row_copy(a).start()

    def send(step, carry):
        target = lax.rem(me + step, peers)
        for a in range(4):
            col_copy(a, target, me).start()
        return carry

    lax.fori_loop(1, peers, send, 0)

    which = lax.broadcasted_iota(jnp.int32, (8, PAIR), 0)
    lane = lax.broadcasted_iota(jnp.int32, (8, PAIR), 1)
    pick = (which == 2 + lane // HD).astype(jnp.float32)
    which_l = lax.broadcasted_iota(jnp.int32, (8, HEADS), 0)
    lane_l = lax.broadcasted_iota(jnp.int32, (8, HEADS), 1)
    sums_row = flat(l_ref[...])
    sums_col = jnp.concatenate((flat(l_ref[:, 0]), flat(l_ref[:, 1])), axis=0)
    exact = functools.partial(
        lax.dot_general, dimension_numbers=NT, precision=lax.Precision.HIGHEST,
        preferred_element_type=jnp.float32,
    )
    for t in range(HEADS // 2):
        part = slice(t * PAIR, (t + 1) * PAIR)
        choose = ((lane_l - 2 * t == which_l) & (which_l < 2)).astype(jnp.float32)
        if t < HEADS // 4:
            products = flat(g_ref[:, :, :, part]) * flat(o_ref[:, :, :, part])
            aux_row[t] = exact(pick, products) + exact(choose, sums_row)
        else:
            products = jnp.concatenate(
                tuple(flat(g_ref[:, s, :, part]) * flat(o_ref[:, s, :, part]) for s in (0, 1)),
                axis=0,
            )
            aux_col[t - HEADS // 4] = exact(pick, products) + exact(choose, sums_col)

    row_aux_copy().start()

    def send_aux(step, carry):
        aux_copy(lax.rem(me + step, peers), me).start()
        return carry

    lax.fori_loop(1, peers, send_aux, 0)
    for a in range(4):
        col_in[a, eight(me)] = ins[a][:, stripe, :, col_lanes(pair)]
    col_aux[me] = aux_col[pair]

    for a in range(4):
        row_copy(a).wait_recv()
    row_aux_copy().wait_recv()
    scratch = (q_s, k_s, v_s, g_s)
    for u in (0, 1):
        part = slice(u * PAIR, (u + 1) * PAIR)
        mine = pl.ds(pl.multiple_of(2 * PAIR * core + u * PAIR, PAIR), PAIR)
        for a in range(4):
            scratch[a][0:128, :] = flat(ins[a][:, :, :, mine]).astype(jnp.bfloat16)
            scratch[a][128:256, :] = flat(row_in[a, :, :, :, part]).astype(jnp.bfloat16)
        rows_s[:, 0:128] = aux_row[2 * core + u]
        rows_s[:, 128:256] = row_aux[u]
        dq = attend(256, 256, q_s, k_s, v_s, g_s, rows_s, dq_t, dk_s, dv_s)
        for a, grads in enumerate((dq, dk_s[0:256, :], dv_s[0:256, :])):
            shaped = grads.reshape((2, 8, 2, 8, PAIR)).astype(jnp.bfloat16)
            outs[a][:, :, :, mine] = shaped[0]
            row_out[a, :, :, :, part] = shaped[1]
    for a in range(3):
        row_back(a, core).start()

    def arrive(step, carry):
        source = lax.rem(me + step, peers)
        for a in range(4):
            col_copy(a, source, source).wait_recv()
        aux_copy(source, source).wait_recv()
        return carry

    lax.fori_loop(1, peers, arrive, 0)
    for a in range(4):
        scratch[a][...] = flat(col_in[a]).astype(jnp.bfloat16)
    low = lane < HD
    for k in range(4):
        first = col_aux[2 * k]
        second = col_aux[2 * k + 1]
        even = jnp.where(low, first, pltpu.roll(second, HD, 1))
        odd = jnp.where(low, pltpu.roll(first, HD, 1), second)
        rows_s[:, k * PAIR : (k + 1) * PAIR] = jnp.where(stripe == 0, even, odd)
    dq = attend(512, 256, q_s, k_s, v_s, g_s, rows_s, dq_t, dk_s, dv_s)
    for a, grads in enumerate((dq, dk_s[...], dv_s[...])):
        col_out[a] = grads.reshape((64, 8, PAIR)).astype(jnp.bfloat16)

    def give(step, carry):
        target = lax.rem(me + step, peers)
        for a in range(3):
            back_copy(a, target, me).start()
        return carry

    lax.fori_loop(1, peers, give, 0)
    for a in range(3):
        outs[a][:, stripe, :, col_lanes(pair)] = col_out[a, eight(me)]

    def finish(step, carry):
        target = lax.rem(me + step, peers)
        for a in range(3):
            back_copy(a, target, target).wait_recv()
        for a in range(3):
            back_copy(a, target, me).wait_send()
        for a in range(4):
            col_copy(a, target, me).wait_send()
        aux_copy(target, me).wait_send()
        return carry

    for a in range(4):
        row_copy(a).wait_send()
    row_aux_copy().wait_send()
    for a in range(3):
        row_back(a, core).wait()
    lax.fori_loop(1, peers, finish, 0)


def local_exchange(peers, queries, key_map, value_map, saved_output, output_grad, saved_logsum):
    rows, cols, width = queries.shape

    def view(values):
        return values.reshape((rows, cols // SW, SW, values.shape[-1]))

    half = jnp.bfloat16
    vmem = pl.BlockSpec(memory_space=pltpu.VMEM)
    dma = pltpu.SemaphoreType.DMA
    grads = pl.pallas_call(
        exchange_kernel,
        out_shape=(jax.ShapeDtypeStruct((rows, cols // SW, SW, width), half),) * 3,
        in_specs=[vmem] * 6,
        out_specs=(vmem,) * 3,
        scratch_shapes=[
            pltpu.VMEM((4, 8 * peers, SW, PAIR), half),
            pltpu.VMEM((peers, 8, PAIR), jnp.float32),
            pltpu.VMEM((4, rows, cols // SW, SW, 2 * PAIR), half),
            pltpu.VMEM((2, 8, PAIR), jnp.float32),
            pltpu.VMEM((4, 8, PAIR), jnp.float32),
            pltpu.VMEM((4, 8, PAIR), jnp.float32),
            pltpu.VMEM((3, 8 * peers, SW, PAIR), half),
            pltpu.VMEM((3, rows, cols // SW, SW, 2 * PAIR), half),
            pltpu.VMEM((512, PAIR), half),
            pltpu.VMEM((512, PAIR), half),
            pltpu.VMEM((512, PAIR), half),
            pltpu.VMEM((512, PAIR), half),
            pltpu.VMEM((8, 512), jnp.float32),
            pltpu.VMEM((PAIR, 512), jnp.float32),
            pltpu.VMEM((512, PAIR), jnp.float32),
            pltpu.VMEM((512, PAIR), jnp.float32),
            dma((4, peers)), dma((4, peers)), dma((peers,)), dma((peers,)),
            dma((5,)), dma((5,)), dma((3, peers)), dma((3, peers)), dma((3,)), dma((3,)),
        ],
        compiler_params=pltpu.CompilerParams(
            collective_id=0, has_side_effects=True, vmem_limit_bytes=40 * 1024 * 1024
        ),
    )(
        view(queries), view(key_map), view(value_map), view(saved_output), view(output_grad),
        view(saved_logsum),
    )
    return tuple(values.astype(jnp.float32).reshape(rows, cols, width) for values in grads)


def local(mesh, *arrays):
    peers = mesh.shape["row"]
    if peers == 8 and mesh.shape["col"] == 2 and arrays[0].shape == (8, 16, HEADS * HD):
        return local_exchange(peers, *arrays)
    return local_general(*arrays)


def solution(mesh):
    in_specs = (
        P(("grp", "row"), "col", None),
        P(("grp", "row"), "col", None),
        P(("grp", "row"), "col", None),
        P(("grp", "row"), "col", None),
        P(("grp", "row"), "col", None),
        P(("grp", "row"), "col", None),
    )
    out_specs = (
        P(("grp", "row"), "col", None),
        P(("grp", "row"), "col", None),
        P(("grp", "row"), "col", None),
    )
    return jax.shard_map(functools.partial(local, mesh), mesh=mesh, in_specs=in_specs, out_specs=out_specs, check_vma=False)
```

```python
import functools
import math

import jax
import jax.numpy as jnp
from jax import lax
from jax.experimental import pallas as pl
from jax.experimental.pallas import tpu as pltpu
from jax.sharding import PartitionSpec as P

HEADS = 16
HD = 64
SW = 8


def attention_terms(
    stripe_query, stripe_key, stripe_value, stripe_grad, stripe_logsum, stripe_delta
):
    scale = 1.0 / math.sqrt(HD)
    scores = (
        jnp.einsum("gahe,gbhe->ghab", stripe_query, stripe_key, preferred_element_type=jnp.float32)
        * scale
    )
    probs = jnp.exp(scores - jnp.swapaxes(stripe_logsum, 1, 2)[..., None])
    grad_probs = jnp.einsum(
        "gahe,gbhe->ghab", stripe_grad, stripe_value, preferred_element_type=jnp.float32
    )
    grad_scores = (probs * (grad_probs - jnp.swapaxes(stripe_delta, 1, 2)[..., None])).astype(
        jnp.bfloat16
    )
    return (probs.astype(jnp.bfloat16), grad_scores)


def query_side(grad_scores, stripe_key):
    total = jnp.einsum(
        "ghab,gbhe->gahe", grad_scores, stripe_key, preferred_element_type=jnp.float32
    )
    return total * (1.0 / math.sqrt(HD))


def key_side(probs_half, grad_scores, stripe_query, stripe_grad):
    key_total = jnp.einsum(
        "ghab,gahe->gbhe", grad_scores, stripe_query, preferred_element_type=jnp.float32
    )
    value_total = jnp.einsum(
        "ghab,gahe->gbhe", probs_half, stripe_grad, preferred_element_type=jnp.float32
    )
    return (key_total * (1.0 / math.sqrt(HD)), value_total)


def in_blocks(step, carry, arrays, size):
    length = arrays[0].shape[0]

    def turn(index, total):
        parts = tuple((lax.dynamic_slice_in_dim(array, index * size, size, 0) for array in arrays))
        return step(total, parts)

    return lax.fori_loop(0, length // size, turn, carry)


def local_general(queries, key_map, value_map, saved_output, output_grad, saved_logsum):
    rows, cols, width = queries.shape
    half = HEADS // 2
    split = half * HD
    tail = (half, HD)
    block = 4 * rows
    products = output_grad.astype(jnp.float32) * saved_output.astype(jnp.float32)
    delta_all = jnp.sum(products.reshape(rows, cols, HEADS, HD), axis=3)

    def row_group(values, last):
        return values.reshape((rows // SW, SW * values.shape[1]) + last)

    def column_group(values, last):
        count = values.shape[0]
        shaped = values.reshape((count, cols // SW, SW) + last)
        return jnp.swapaxes(shaped, 0, 1).reshape((cols // SW, count * SW) + last)

    def column_back(values, count):
        shaped = values.reshape((cols // SW, count, SW, -1))
        return jnp.swapaxes(shaped, 0, 1).reshape(count, cols, -1)

    full_key, full_value = (
        lax.all_gather(key_map[:, :, :split], "col", axis=1, tiled=True),
        lax.all_gather(value_map[:, :, :split], "col", axis=1, tiled=True),
    )
    wide = full_key.shape[1]
    stripe_query = row_group(queries[:, :, :split], tail)
    stripe_grad = row_group(output_grad[:, :, :split], tail)
    stripe_logsum = row_group(saved_logsum[:, :, :half], (half,))
    stripe_delta = row_group(delta_all[:, :, :half], (half,))
    stripe_key = row_group(full_key, tail)
    stripe_value = row_group(full_value, tail)
    probs_half, grad_scores = attention_terms(
        stripe_query, stripe_key, stripe_value, stripe_grad, stripe_logsum, stripe_delta
    )
    row_query_grad = query_side(grad_scores, stripe_key).reshape(rows, cols, split)
    row_key_part, row_value_part = key_side(probs_half, grad_scores, stripe_query, stripe_grad)
    row_term = jnp.concatenate(
        (row_key_part.reshape(rows, wide, split), row_value_part.reshape(rows, wide, split)), axis=2
    )
    row_sums = lax.psum_scatter(row_term, "col", scatter_dimension=1, tiled=True)
    local_key = key_map[:, :, split:]
    local_value = value_map[:, :, split:]
    column_query = column_group(queries[:, :, split:], tail)
    column_grad = column_group(output_grad[:, :, split:], tail)
    column_logsum = column_group(saved_logsum[:, :, half:], (half,))
    column_delta = column_group(delta_all[:, :, half:], (half,))

    def query_step(total, pieces):
        grouped_key = column_group(pieces[0], tail)
        grouped_value = column_group(pieces[1], tail)
        weights, gradients = attention_terms(
            column_query, grouped_key, grouped_value, column_grad, column_logsum, column_delta
        )
        return total + query_side(gradients, grouped_key)

    empty_query = jnp.zeros(column_query.shape, jnp.float32)
    every_key, every_value = (
        lax.all_gather(local_key, "row", axis=0, tiled=True),
        lax.all_gather(local_value, "row", axis=0, tiled=True),
    )
    column_total = in_blocks(query_step, empty_query, (every_key, every_value), block)

    def key_step(pieces):
        count = pieces[0].shape[0]
        grouped_key = column_group(pieces[0], tail)
        grouped_value = column_group(pieces[1], tail)
        weights, gradients = attention_terms(
            column_query, grouped_key, grouped_value, column_grad, column_logsum, column_delta
        )
        key_part, value_part = key_side(weights, gradients, column_query, column_grad)
        return jnp.concatenate(
            (column_back(key_part, count), column_back(value_part, count)), axis=2
        )

    count = rows * lax.axis_size("row")
    stacked = lax.map(
        key_step,
        (
            every_key.reshape((count // block, block) + every_key.shape[1:]),
            every_value.reshape((count // block, block) + every_value.shape[1:]),
        ),
    )
    column_sums = lax.psum_scatter(
        stacked.reshape((count,) + stacked.shape[2:]), "row", scatter_dimension=0, tiled=True
    )
    column_key_grad = column_sums[:, :, :split]
    column_value_grad = column_sums[:, :, split:]
    column_query_grad = column_back(column_total, rows)
    query_grad = jnp.concatenate((row_query_grad, column_query_grad), axis=2)
    key_grad = jnp.concatenate((row_sums[:, :, :split], column_key_grad), axis=2)
    value_grad = jnp.concatenate((row_sums[:, :, split:], column_value_grad), axis=2)
    return (query_grad, key_grad, value_grad)


MESH = pl.DeviceIdType.MESH
NT = (((1,), (1,)), ((), ()))
TN = (((0,), (0,)), ((), ()))
PAIR = 2 * HD


def flat(values):
    return values.astype(jnp.float32).reshape((-1, values.shape[-1]))


def attend(count, block, q_s, k_s, v_s, g_s, rows, dq_t, dk_s, dv_s):
    scale = 1.0 / math.sqrt(HD)
    lane = lax.broadcasted_iota(jnp.int32, (block, PAIR), 1)
    masks = tuple(((lane // HD) == h).astype(jnp.float32).astype(jnp.bfloat16) for h in (0, 1))

    def step(j, carry):
        part = pl.ds(pl.multiple_of(j * block, block), block)
        q = q_s[0:count, :]
        g = g_s[0:count, :]
        keys = k_s[part, :]
        values = v_s[part, :]
        dk = []
        dv = []
        dq = None
        for h in (0, 1):
            key = keys * masks[h]
            value = values * masks[h]
            scores = lax.dot_general(key, q, NT, preferred_element_type=jnp.float32)
            probs = jnp.exp(scores * scale - rows[h : h + 1, 0:count])
            grad_probs = lax.dot_general(value, g, NT, preferred_element_type=jnp.float32)
            grad_scores = (probs * (grad_probs - rows[2 + h : 3 + h, 0:count])).astype(jnp.bfloat16)
            half = probs.astype(jnp.bfloat16)
            dv.append(jnp.dot(half, g, preferred_element_type=jnp.float32))
            dk.append(jnp.dot(grad_scores, q, preferred_element_type=jnp.float32))
            term = lax.dot_general(key, grad_scores, TN, preferred_element_type=jnp.float32)
            dq = term if dq is None else dq + term
        dk_s[part, :] = jnp.where(lane < HD, dk[0], dk[1]) * scale
        dv_s[part, :] = jnp.where(lane < HD, dv[0], dv[1])
        dq_t[:, 0:count] += dq
        return carry

    dq_t[:, 0:count] = jnp.zeros((PAIR, count), jnp.float32)
    lax.fori_loop(0, count // block, step, 0)
    return dq_t[:, 0:count].T * scale


def exchange_kernel(
    q_hbm, k_hbm, v_hbm, o_hbm, g_hbm, l_hbm,
    dq_ref, dk_ref, dv_ref,
    col_in, col_aux, row_in, row_aux, aux_row, aux_col, col_out, row_out,
    q_s, k_s, v_s, g_s, rows_s, dq_t, dk_s, dv_s,
    q_ref, k_ref, v_ref, o_ref, g_ref, l_ref, in_sem,
    cs_sem, cr_sem, as_sem, ar_sem, rs_sem, rr_sem, os_sem, or_sem, ps_sem, pr_sem,
):
    me = lax.axis_index("row")
    core = lax.axis_index("col")
    peers = lax.axis_size("row")
    other = 1 - core
    split = (HEADS // 2) * HD
    pair = me // 2
    stripe = me % 2
    ins = (q_ref, k_ref, v_ref, g_ref)
    outs = (dq_ref, dk_ref, dv_ref)
    sources = (q_hbm, k_hbm, v_hbm, g_hbm)
    loads = [
        pltpu.make_async_copy(source, target, in_sem.at[n])
        for n, (source, target) in enumerate(
            (
                (g_hbm, g_ref), (o_hbm, o_ref), (l_hbm, l_ref),
                (q_hbm, q_ref), (k_hbm, k_ref), (v_hbm, v_ref),
            )
        )
    ]
    for load in loads:
        load.start()

    barrier = pltpu.get_barrier_semaphore()
    for step in range(1, peers):
        pl.semaphore_signal(
            barrier, inc=1, device_id={"row": lax.rem(me + step, peers)}, device_id_type=MESH
        )
    pl.semaphore_signal(barrier, inc=1, device_id={"col": other}, device_id_type=MESH)
    pl.semaphore_wait(barrier, peers)

    def col_lanes(index):
        return pl.ds(pl.multiple_of(split + PAIR * index, PAIR), PAIR)

    def core_lanes(index):
        return pl.ds(pl.multiple_of(2 * PAIR * index, 2 * PAIR), 2 * PAIR)

    def eight(index):
        return pl.ds(pl.multiple_of(index * 8, 8), 8)

    def row_copy(a):
        return pltpu.make_async_remote_copy(
            src_ref=sources[a].at[:, :, :, core_lanes(other)],
            dst_ref=row_in.at[a],
            send_sem=rs_sem.at[a], recv_sem=rr_sem.at[a],
            device_id={"col": other}, device_id_type=MESH,
        )

    def col_copy(a, target, source):
        return pltpu.make_async_remote_copy(
            src_ref=sources[a].at[:, target % 2, :, col_lanes(target // 2)],
            dst_ref=col_in.at[a, eight(source)],
            send_sem=cs_sem.at[a, target], recv_sem=cr_sem.at[a, source],
            device_id={"row": target}, device_id_type=MESH,
        )

    def aux_copy(target, source):
        return pltpu.make_async_remote_copy(
            src_ref=aux_col.at[target // 2],
            dst_ref=col_aux.at[source],
            send_sem=as_sem.at[target], recv_sem=ar_sem.at[source],
            device_id={"row": target}, device_id_type=MESH,
        )

    def back_copy(a, target, owner):
        return pltpu.make_async_remote_copy(
            src_ref=col_out.at[a, eight(target)],
            dst_ref=outs[a].at[:, owner % 2, :, col_lanes(owner // 2)],
            send_sem=os_sem.at[a, target], recv_sem=or_sem.at[a, owner],
            device_id={"row": target}, device_id_type=MESH,
        )

    def row_back(a, owner):
        return pltpu.make_async_remote_copy(
            src_ref=row_out.at[a],
            dst_ref=outs[a].at[:, :, :, core_lanes(owner)],
            send_sem=ps_sem.at[a], recv_sem=pr_sem.at[a],
            device_id={"col": other}, device_id_type=MESH,
        )

    def row_aux_copy():
        return pltpu.make_async_remote_copy(
            src_ref=aux_row.at[pl.ds(2 * other, 2)],
            dst_ref=row_aux,
            send_sem=rs_sem.at[4], recv_sem=rr_sem.at[4],
            device_id={"col": other}, device_id_type=MESH,
        )

    for a in range(4):
        row_copy(a).start()

    def partner(step):
        flip = jnp.where(step < 5, step + 3, step - 4)
        return (me // 4 + flip // 4) % 2 * 4 + (me // 2 + flip // 2) % 2 * 2 + (me + flip) % 2

    def send(step, carry):
        target = partner(step)
        for a in range(4):
            col_copy(a, target, me).start()
        return carry

    lax.fori_loop(1, peers, send, 0)

    for load in loads[:3]:
        load.wait()
    which = lax.broadcasted_iota(jnp.int32, (8, PAIR), 0)
    lane = lax.broadcasted_iota(jnp.int32, (8, PAIR), 1)
    pick = (which == 2 + lane // HD).astype(jnp.float32)
    which_l = lax.broadcasted_iota(jnp.int32, (8, HEADS), 0)
    lane_l = lax.broadcasted_iota(jnp.int32, (8, HEADS), 1)
    sums_row = flat(l_ref[...])
    sums_col = jnp.concatenate((flat(l_ref[:, 0]), flat(l_ref[:, 1])), axis=0)
    exact = functools.partial(
        lax.dot_general, dimension_numbers=NT, precision=lax.Precision.HIGHEST,
        preferred_element_type=jnp.float32,
    )
    for t in range(HEADS // 2):
        part = slice(t * PAIR, (t + 1) * PAIR)
        choose = ((lane_l - 2 * t == which_l) & (which_l < 2)).astype(jnp.float32)
        if t < HEADS // 4:
            products = flat(g_ref[:, :, :, part]) * flat(o_ref[:, :, :, part])
            aux_row[t] = exact(pick, products) + exact(choose, sums_row)
        else:
            products = jnp.concatenate(
                tuple(flat(g_ref[:, s, :, part]) * flat(o_ref[:, s, :, part]) for s in (0, 1)),
                axis=0,
            )
            aux_col[t - HEADS // 4] = exact(pick, products) + exact(choose, sums_col)

    row_aux_copy().start()

    def send_aux(step, carry):
        aux_copy(partner(step), me).start()
        return carry

    lax.fori_loop(1, peers, send_aux, 0)
    for load in loads[3:]:
        load.wait()
    for a in range(4):
        col_in[a, eight(me)] = ins[a][:, stripe, :, col_lanes(pair)]
    col_aux[me] = aux_col[pair]

    for a in range(4):
        row_copy(a).wait_recv()
    row_aux_copy().wait_recv()
    scratch = (q_s, k_s, v_s, g_s)
    for u in (0, 1):
        part = slice(u * PAIR, (u + 1) * PAIR)
        mine = pl.ds(pl.multiple_of(2 * PAIR * core + u * PAIR, PAIR), PAIR)
        for a in range(4):
            scratch[a][0:128, :] = flat(ins[a][:, :, :, mine]).astype(jnp.bfloat16)
            scratch[a][128:256, :] = flat(row_in[a, :, :, :, part]).astype(jnp.bfloat16)
        rows_s[:, 0:128] = aux_row[2 * core + u]
        rows_s[:, 128:256] = row_aux[u]
        dq = attend(256, 256, q_s, k_s, v_s, g_s, rows_s, dq_t, dk_s, dv_s)
        for a, grads in enumerate((dq, dk_s[0:256, :], dv_s[0:256, :])):
            shaped = grads.reshape((2, 8, 2, 8, PAIR)).astype(jnp.bfloat16)
            outs[a][:, :, :, mine] = shaped[0]
            row_out[a, :, :, :, part] = shaped[1]
    for a in range(3):
        row_back(a, core).start()

    def arrive(step, carry):
        source = partner(step)
        for a in range(4):
            col_copy(a, source, source).wait_recv()
        aux_copy(source, source).wait_recv()
        return carry

    lax.fori_loop(1, peers, arrive, 0)
    for a in range(4):
        scratch[a][...] = flat(col_in[a]).astype(jnp.bfloat16)
    low = lane < HD
    for k in range(4):
        first = col_aux[2 * k]
        second = col_aux[2 * k + 1]
        even = jnp.where(low, first, pltpu.roll(second, HD, 1))
        odd = jnp.where(low, pltpu.roll(first, HD, 1), second)
        rows_s[:, k * PAIR : (k + 1) * PAIR] = jnp.where(stripe == 0, even, odd)
    dq = attend(512, 256, q_s, k_s, v_s, g_s, rows_s, dq_t, dk_s, dv_s)
    for a, grads in enumerate((dq, dk_s[...], dv_s[...])):
        col_out[a] = grads.reshape((64, 8, PAIR)).astype(jnp.bfloat16)

    def give(step, carry):
        target = partner(step)
        for a in range(3):
            back_copy(a, target, me).start()
        return carry

    lax.fori_loop(1, peers, give, 0)
    for a in range(3):
        outs[a][:, stripe, :, col_lanes(pair)] = col_out[a, eight(me)]

    def finish(step, carry):
        target = partner(step)
        for a in range(3):
            back_copy(a, target, target).wait_recv()
        for a in range(3):
            back_copy(a, target, me).wait_send()
        for a in range(4):
            col_copy(a, target, me).wait_send()
        aux_copy(target, me).wait_send()
        return carry

    for a in range(4):
        row_copy(a).wait_send()
    row_aux_copy().wait_send()
    for a in range(3):
        row_back(a, core).wait()
    lax.fori_loop(1, peers, finish, 0)


def local_exchange(peers, queries, key_map, value_map, saved_output, output_grad, saved_logsum):
    rows, cols, width = queries.shape

    def view(values):
        return values.reshape((rows, cols // SW, SW, values.shape[-1]))

    half = jnp.bfloat16
    vmem = pl.BlockSpec(memory_space=pltpu.VMEM)
    dma = pltpu.SemaphoreType.DMA
    grads = pl.pallas_call(
        exchange_kernel,
        out_shape=(jax.ShapeDtypeStruct((rows, cols // SW, SW, width), half),) * 3,
        in_specs=[pl.BlockSpec(memory_space=pltpu.HBM)] * 6,
        out_specs=(vmem,) * 3,
        scratch_shapes=[
            pltpu.VMEM((4, 8 * peers, SW, PAIR), half),
            pltpu.VMEM((peers, 8, PAIR), jnp.float32),
            pltpu.VMEM((4, rows, cols // SW, SW, 2 * PAIR), half),
            pltpu.VMEM((2, 8, PAIR), jnp.float32),
            pltpu.VMEM((4, 8, PAIR), jnp.float32),
            pltpu.VMEM((4, 8, PAIR), jnp.float32),
            pltpu.VMEM((3, 8 * peers, SW, PAIR), half),
            pltpu.VMEM((3, rows, cols // SW, SW, 2 * PAIR), half),
            pltpu.VMEM((512, PAIR), half),
            pltpu.VMEM((512, PAIR), half),
            pltpu.VMEM((512, PAIR), half),
            pltpu.VMEM((512, PAIR), half),
            pltpu.VMEM((8, 512), jnp.float32),
            pltpu.VMEM((PAIR, 512), jnp.float32),
            pltpu.VMEM((512, PAIR), jnp.float32),
            pltpu.VMEM((512, PAIR), jnp.float32),
            *(pltpu.VMEM((rows, cols // SW, SW, width), half) for _ in range(5)),
            pltpu.VMEM((rows, cols // SW, SW, HEADS), jnp.float32),
            dma((6,)),
            dma((4, peers)), dma((4, peers)), dma((peers,)), dma((peers,)),
            dma((5,)), dma((5,)), dma((3, peers)), dma((3, peers)), dma((3,)), dma((3,)),
        ],
        compiler_params=pltpu.CompilerParams(
            collective_id=0, has_side_effects=True, vmem_limit_bytes=40 * 1024 * 1024
        ),
    )(
        view(queries), view(key_map), view(value_map), view(saved_output), view(output_grad),
        view(saved_logsum),
    )
    return tuple(values.astype(jnp.float32).reshape(rows, cols, width) for values in grads)


def local(mesh, *arrays):
    peers = mesh.shape["row"]
    if peers == 8 and mesh.shape["col"] == 2 and arrays[0].shape == (8, 16, HEADS * HD):
        return local_exchange(peers, *arrays)
    return local_general(*arrays)


def solution(mesh):
    in_specs = (
        P(("grp", "row"), "col", None),
        P(("grp", "row"), "col", None),
        P(("grp", "row"), "col", None),
        P(("grp", "row"), "col", None),
        P(("grp", "row"), "col", None),
        P(("grp", "row"), "col", None),
    )
    out_specs = (
        P(("grp", "row"), "col", None),
        P(("grp", "row"), "col", None),
        P(("grp", "row"), "col", None),
    )
    return jax.shard_map(functools.partial(local, mesh), mesh=mesh, in_specs=in_specs, out_specs=out_specs, check_vma=False)
```

```python
import functools
import math

import jax
import jax.numpy as jnp
from jax import lax
from jax.experimental import pallas as pl
from jax.experimental.pallas import tpu as pltpu
from jax.sharding import PartitionSpec as P

HEADS = 16
HD = 64
SW = 8


def attention_terms(
    stripe_query, stripe_key, stripe_value, stripe_grad, stripe_logsum, stripe_delta
):
    scale = 1.0 / math.sqrt(HD)
    scores = (
        jnp.einsum("gahe,gbhe->ghab", stripe_query, stripe_key, preferred_element_type=jnp.float32)
        * scale
    )
    probs = jnp.exp(scores - jnp.swapaxes(stripe_logsum, 1, 2)[..., None])
    grad_probs = jnp.einsum(
        "gahe,gbhe->ghab", stripe_grad, stripe_value, preferred_element_type=jnp.float32
    )
    grad_scores = (probs * (grad_probs - jnp.swapaxes(stripe_delta, 1, 2)[..., None])).astype(
        jnp.bfloat16
    )
    return (probs.astype(jnp.bfloat16), grad_scores)


def query_side(grad_scores, stripe_key):
    total = jnp.einsum(
        "ghab,gbhe->gahe", grad_scores, stripe_key, preferred_element_type=jnp.float32
    )
    return total * (1.0 / math.sqrt(HD))


def key_side(probs_half, grad_scores, stripe_query, stripe_grad):
    key_total = jnp.einsum(
        "ghab,gahe->gbhe", grad_scores, stripe_query, preferred_element_type=jnp.float32
    )
    value_total = jnp.einsum(
        "ghab,gahe->gbhe", probs_half, stripe_grad, preferred_element_type=jnp.float32
    )
    return (key_total * (1.0 / math.sqrt(HD)), value_total)


def in_blocks(step, carry, arrays, size):
    length = arrays[0].shape[0]

    def turn(index, total):
        parts = tuple((lax.dynamic_slice_in_dim(array, index * size, size, 0) for array in arrays))
        return step(total, parts)

    return lax.fori_loop(0, length // size, turn, carry)


def local_general(queries, key_map, value_map, saved_output, output_grad, saved_logsum):
    rows, cols, width = queries.shape
    half = HEADS // 2
    split = half * HD
    tail = (half, HD)
    block = 4 * rows
    products = output_grad.astype(jnp.float32) * saved_output.astype(jnp.float32)
    delta_all = jnp.sum(products.reshape(rows, cols, HEADS, HD), axis=3)

    def row_group(values, last):
        return values.reshape((rows // SW, SW * values.shape[1]) + last)

    def column_group(values, last):
        count = values.shape[0]
        shaped = values.reshape((count, cols // SW, SW) + last)
        return jnp.swapaxes(shaped, 0, 1).reshape((cols // SW, count * SW) + last)

    def column_back(values, count):
        shaped = values.reshape((cols // SW, count, SW, -1))
        return jnp.swapaxes(shaped, 0, 1).reshape(count, cols, -1)

    full_key, full_value = (
        lax.all_gather(key_map[:, :, :split], "col", axis=1, tiled=True),
        lax.all_gather(value_map[:, :, :split], "col", axis=1, tiled=True),
    )
    wide = full_key.shape[1]
    stripe_query = row_group(queries[:, :, :split], tail)
    stripe_grad = row_group(output_grad[:, :, :split], tail)
    stripe_logsum = row_group(saved_logsum[:, :, :half], (half,))
    stripe_delta = row_group(delta_all[:, :, :half], (half,))
    stripe_key = row_group(full_key, tail)
    stripe_value = row_group(full_value, tail)
    probs_half, grad_scores = attention_terms(
        stripe_query, stripe_key, stripe_value, stripe_grad, stripe_logsum, stripe_delta
    )
    row_query_grad = query_side(grad_scores, stripe_key).reshape(rows, cols, split)
    row_key_part, row_value_part = key_side(probs_half, grad_scores, stripe_query, stripe_grad)
    row_term = jnp.concatenate(
        (row_key_part.reshape(rows, wide, split), row_value_part.reshape(rows, wide, split)), axis=2
    )
    row_sums = lax.psum_scatter(row_term, "col", scatter_dimension=1, tiled=True)
    local_key = key_map[:, :, split:]
    local_value = value_map[:, :, split:]
    column_query = column_group(queries[:, :, split:], tail)
    column_grad = column_group(output_grad[:, :, split:], tail)
    column_logsum = column_group(saved_logsum[:, :, half:], (half,))
    column_delta = column_group(delta_all[:, :, half:], (half,))

    def query_step(total, pieces):
        grouped_key = column_group(pieces[0], tail)
        grouped_value = column_group(pieces[1], tail)
        weights, gradients = attention_terms(
            column_query, grouped_key, grouped_value, column_grad, column_logsum, column_delta
        )
        return total + query_side(gradients, grouped_key)

    empty_query = jnp.zeros(column_query.shape, jnp.float32)
    every_key, every_value = (
        lax.all_gather(local_key, "row", axis=0, tiled=True),
        lax.all_gather(local_value, "row", axis=0, tiled=True),
    )
    column_total = in_blocks(query_step, empty_query, (every_key, every_value), block)

    def key_step(pieces):
        count = pieces[0].shape[0]
        grouped_key = column_group(pieces[0], tail)
        grouped_value = column_group(pieces[1], tail)
        weights, gradients = attention_terms(
            column_query, grouped_key, grouped_value, column_grad, column_logsum, column_delta
        )
        key_part, value_part = key_side(weights, gradients, column_query, column_grad)
        return jnp.concatenate(
            (column_back(key_part, count), column_back(value_part, count)), axis=2
        )

    count = rows * lax.axis_size("row")
    stacked = lax.map(
        key_step,
        (
            every_key.reshape((count // block, block) + every_key.shape[1:]),
            every_value.reshape((count // block, block) + every_value.shape[1:]),
        ),
    )
    column_sums = lax.psum_scatter(
        stacked.reshape((count,) + stacked.shape[2:]), "row", scatter_dimension=0, tiled=True
    )
    column_key_grad = column_sums[:, :, :split]
    column_value_grad = column_sums[:, :, split:]
    column_query_grad = column_back(column_total, rows)
    query_grad = jnp.concatenate((row_query_grad, column_query_grad), axis=2)
    key_grad = jnp.concatenate((row_sums[:, :, :split], column_key_grad), axis=2)
    value_grad = jnp.concatenate((row_sums[:, :, split:], column_value_grad), axis=2)
    return (query_grad, key_grad, value_grad)


MESH = pl.DeviceIdType.MESH
NT = (((1,), (1,)), ((), ()))
TN = (((0,), (0,)), ((), ()))
PAIR = 2 * HD


def flat(values):
    return values.astype(jnp.float32).reshape((-1, values.shape[-1]))


def attend(count, block, q_s, k_s, v_s, g_s, rows, dq_t, dk_s, dv_s):
    scale = 1.0 / math.sqrt(HD)
    lane = lax.broadcasted_iota(jnp.int32, (block, PAIR), 1)
    masks = tuple(((lane // HD) == h).astype(jnp.float32).astype(jnp.bfloat16) for h in (0, 1))

    def step(j, carry):
        part = pl.ds(pl.multiple_of(j * block, block), block)
        q = q_s[0:count, :]
        g = g_s[0:count, :]
        keys = k_s[part, :]
        values = v_s[part, :]
        dk = []
        dv = []
        dq = None
        for h in (0, 1):
            key = keys * masks[h]
            value = values * masks[h]
            scores = lax.dot_general(key, q, NT, preferred_element_type=jnp.float32)
            probs = jnp.exp(scores * scale - rows[h : h + 1, 0:count])
            grad_probs = lax.dot_general(value, g, NT, preferred_element_type=jnp.float32)
            grad_scores = (probs * (grad_probs - rows[2 + h : 3 + h, 0:count])).astype(jnp.bfloat16)
            half = probs.astype(jnp.bfloat16)
            dv.append(jnp.dot(half, g, preferred_element_type=jnp.float32))
            dk.append(jnp.dot(grad_scores, q, preferred_element_type=jnp.float32))
            term = lax.dot_general(key, grad_scores, TN, preferred_element_type=jnp.float32)
            dq = term if dq is None else dq + term
        dk_s[part, :] = jnp.where(lane < HD, dk[0], dk[1]) * scale
        dv_s[part, :] = jnp.where(lane < HD, dv[0], dv[1])
        dq_t[:, 0:count] += dq
        return carry

    dq_t[:, 0:count] = jnp.zeros((PAIR, count), jnp.float32)
    lax.fori_loop(0, count // block, step, 0)
    return dq_t[:, 0:count].T * scale


def exchange_kernel(
    q_hbm, k_hbm, v_hbm, o_hbm, g_hbm, l_hbm,
    dq_ref, dk_ref, dv_ref,
    col_in, col_aux, row_in, row_aux, aux_row, aux_col, col_out, row_out,
    q_s, k_s, v_s, g_s, rows_s, dq_t, dk_s, dv_s,
    q_ref, k_ref, v_ref, o_ref, g_ref, l_ref, in_sem,
    cs_sem, cr_sem, as_sem, ar_sem, rs_sem, rr_sem, os_sem, or_sem, ps_sem, pr_sem,
):
    me = lax.axis_index("row")
    core = lax.axis_index("col")
    peers = lax.axis_size("row")
    other = 1 - core
    split = (HEADS // 2) * HD
    pair = me // 2
    stripe = me % 2
    ins = (q_ref, k_ref, v_ref, g_ref)
    outs = (dq_ref, dk_ref, dv_ref)
    sources = (q_hbm, k_hbm, v_hbm, g_hbm)
    loads = [
        pltpu.make_async_copy(source, target, in_sem.at[n])
        for n, (source, target) in enumerate(
            (
                (g_hbm, g_ref), (o_hbm, o_ref), (l_hbm, l_ref),
                (q_hbm, q_ref), (k_hbm, k_ref), (v_hbm, v_ref),
            )
        )
    ]
    for load in loads:
        load.start()

    barrier = pltpu.get_barrier_semaphore()
    for step in range(1, peers):
        pl.semaphore_signal(
            barrier, inc=1, device_id={"row": lax.rem(me + step, peers)}, device_id_type=MESH
        )
    pl.semaphore_signal(barrier, inc=1, device_id={"col": other}, device_id_type=MESH)
    pl.semaphore_wait(barrier, peers)

    def col_lanes(index):
        return pl.ds(pl.multiple_of(split + PAIR * index, PAIR), PAIR)

    def core_lanes(index):
        return pl.ds(pl.multiple_of(2 * PAIR * index, 2 * PAIR), 2 * PAIR)

    def eight(index):
        return pl.ds(pl.multiple_of(index * 8, 8), 8)

    def row_copy(a):
        return pltpu.make_async_remote_copy(
            src_ref=sources[a].at[:, :, :, core_lanes(other)],
            dst_ref=row_in.at[a],
            send_sem=rs_sem.at[a], recv_sem=rr_sem.at[a],
            device_id={"col": other}, device_id_type=MESH,
        )

    def col_copy(a, target, source):
        return pltpu.make_async_remote_copy(
            src_ref=sources[a].at[:, target % 2, :, col_lanes(target // 2)],
            dst_ref=col_in.at[a, eight(source)],
            send_sem=cs_sem.at[a, target], recv_sem=cr_sem.at[a, source],
            device_id={"row": target}, device_id_type=MESH,
        )

    def aux_copy(target, source):
        return pltpu.make_async_remote_copy(
            src_ref=aux_col.at[target // 2],
            dst_ref=col_aux.at[source],
            send_sem=as_sem.at[target], recv_sem=ar_sem.at[source],
            device_id={"row": target}, device_id_type=MESH,
        )

    def back_copy(a, target, owner):
        return pltpu.make_async_remote_copy(
            src_ref=col_out.at[a, eight(target)],
            dst_ref=outs[a].at[:, owner % 2, :, col_lanes(owner // 2)],
            send_sem=os_sem.at[a, target], recv_sem=or_sem.at[a, owner],
            device_id={"row": target}, device_id_type=MESH,
        )

    def row_back(a, owner):
        return pltpu.make_async_remote_copy(
            src_ref=row_out.at[a],
            dst_ref=outs[a].at[:, :, :, core_lanes(owner)],
            send_sem=ps_sem.at[a], recv_sem=pr_sem.at[a],
            device_id={"col": other}, device_id_type=MESH,
        )

    def row_aux_copy():
        return pltpu.make_async_remote_copy(
            src_ref=aux_row.at[pl.ds(2 * other, 2)],
            dst_ref=row_aux,
            send_sem=rs_sem.at[4], recv_sem=rr_sem.at[4],
            device_id={"col": other}, device_id_type=MESH,
        )

    for a in range(4):
        row_copy(a).start()

    def partner(step):
        flip = jnp.where(step < 5, step + 3, step - 4)
        return (me // 4 + flip // 4) % 2 * 4 + (me // 2 + flip // 2) % 2 * 2 + (me + flip) % 2

    def send(step, carry):
        target = partner(step)
        for a in range(4):
            col_copy(a, target, me).start()
        return carry

    lax.fori_loop(1, peers, send, 0)

    for load in loads[:3]:
        load.wait()
    which = lax.broadcasted_iota(jnp.int32, (8, PAIR), 0)
    lane = lax.broadcasted_iota(jnp.int32, (8, PAIR), 1)
    pick = (which == 2 + lane // HD).astype(jnp.float32)
    which_l = lax.broadcasted_iota(jnp.int32, (8, HEADS), 0)
    lane_l = lax.broadcasted_iota(jnp.int32, (8, HEADS), 1)
    sums_row = flat(l_ref[...])
    sums_col = jnp.concatenate((flat(l_ref[:, 0]), flat(l_ref[:, 1])), axis=0)
    exact = functools.partial(
        lax.dot_general, dimension_numbers=NT, precision=lax.Precision.HIGHEST,
        preferred_element_type=jnp.float32,
    )
    for t in range(HEADS // 2):
        part = slice(t * PAIR, (t + 1) * PAIR)
        choose = ((lane_l - 2 * t == which_l) & (which_l < 2)).astype(jnp.float32)
        if t < HEADS // 4:
            products = flat(g_ref[:, :, :, part]) * flat(o_ref[:, :, :, part])
            aux_row[t] = exact(pick, products) + exact(choose, sums_row)
        else:
            products = jnp.concatenate(
                tuple(flat(g_ref[:, s, :, part]) * flat(o_ref[:, s, :, part]) for s in (0, 1)),
                axis=0,
            )
            aux_col[t - HEADS // 4] = exact(pick, products) + exact(choose, sums_col)

    row_aux_copy().start()

    def send_aux(step, carry):
        aux_copy(partner(step), me).start()
        return carry

    lax.fori_loop(1, peers, send_aux, 0)
    for load in loads[3:]:
        load.wait()
    for a in range(4):
        col_in[a, eight(me)] = ins[a][:, stripe, :, col_lanes(pair)]
    col_aux[me] = aux_col[pair]

    for a in range(4):
        row_copy(a).wait_recv()
    row_aux_copy().wait_recv()
    scratch = (q_s, k_s, v_s, g_s)
    for u in (0, 1):
        part = slice(u * PAIR, (u + 1) * PAIR)
        mine = pl.ds(pl.multiple_of(2 * PAIR * core + u * PAIR, PAIR), PAIR)
        for a in range(4):
            scratch[a][0:128, :] = flat(ins[a][:, :, :, mine]).astype(jnp.bfloat16)
            scratch[a][128:256, :] = flat(row_in[a, :, :, :, part]).astype(jnp.bfloat16)
        rows_s[:, 0:128] = aux_row[2 * core + u]
        rows_s[:, 128:256] = row_aux[u]
        dq = attend(256, 256, q_s, k_s, v_s, g_s, rows_s, dq_t, dk_s, dv_s)
        for a, grads in enumerate((dq, dk_s[0:256, :], dv_s[0:256, :])):
            shaped = grads.reshape((2, 8, 2, 8, PAIR)).astype(jnp.bfloat16)
            outs[a][:, :, :, mine] = shaped[0]
            row_out[a, :, :, :, part] = shaped[1]
    for a in range(3):
        row_back(a, core).start()

    def arrive(step, carry):
        source = partner(step)
        for a in range(4):
            col_copy(a, source, source).wait_recv()
        aux_copy(source, source).wait_recv()
        return carry

    lax.fori_loop(1, peers, arrive, 0)
    for a in range(4):
        scratch[a][...] = flat(col_in[a]).astype(jnp.bfloat16)
    low = lane < HD
    for k in range(4):
        first = col_aux[2 * k]
        second = col_aux[2 * k + 1]
        even = jnp.where(low, first, pltpu.roll(second, HD, 1))
        odd = jnp.where(low, pltpu.roll(first, HD, 1), second)
        rows_s[:, k * PAIR : (k + 1) * PAIR] = jnp.where(stripe == 0, even, odd)
    dq = attend(512, 256, q_s, k_s, v_s, g_s, rows_s, dq_t, dk_s, dv_s)
    for a, grads in enumerate((dq, dk_s[...], dv_s[...])):
        col_out[a] = grads.reshape((64, 8, PAIR)).astype(jnp.bfloat16)

    def give(step, carry):
        target = partner(step)
        for a in range(3):
            back_copy(a, target, me).start()
        return carry

    lax.fori_loop(1, peers, give, 0)
    for a in range(3):
        outs[a][:, stripe, :, col_lanes(pair)] = col_out[a, eight(me)]

    def finish(step, carry):
        target = partner(step)
        for a in range(3):
            back_copy(a, target, target).wait_recv()
        for a in range(3):
            back_copy(a, target, me).wait_send()
        for a in range(4):
            col_copy(a, target, me).wait_send()
        aux_copy(target, me).wait_send()
        return carry

    for a in range(4):
        row_copy(a).wait_send()
    row_aux_copy().wait_send()
    for a in range(3):
        row_back(a, core).wait()
    lax.fori_loop(1, peers, finish, 0)


def local_exchange(peers, queries, key_map, value_map, saved_output, output_grad, saved_logsum):
    rows, cols, width = queries.shape

    def view(values):
        return values.reshape((rows, cols // SW, SW, values.shape[-1]))

    half = jnp.bfloat16
    vmem = pl.BlockSpec(memory_space=pltpu.VMEM)
    dma = pltpu.SemaphoreType.DMA
    grads = pl.pallas_call(
        exchange_kernel,
        out_shape=(jax.ShapeDtypeStruct((rows, cols // SW, SW, width), half),) * 3,
        in_specs=[pl.BlockSpec(memory_space=pltpu.HBM)] * 6,
        out_specs=(vmem,) * 3,
        scratch_shapes=[
            pltpu.VMEM((4, 8 * peers, SW, PAIR), half),
            pltpu.VMEM((peers, 8, PAIR), jnp.float32),
            pltpu.VMEM((4, rows, cols // SW, SW, 2 * PAIR), half),
            pltpu.VMEM((2, 8, PAIR), jnp.float32),
            pltpu.VMEM((4, 8, PAIR), jnp.float32),
            pltpu.VMEM((4, 8, PAIR), jnp.float32),
            pltpu.VMEM((3, 8 * peers, SW, PAIR), half),
            pltpu.VMEM((3, rows, cols // SW, SW, 2 * PAIR), half),
            pltpu.VMEM((512, PAIR), half),
            pltpu.VMEM((512, PAIR), half),
            pltpu.VMEM((512, PAIR), half),
            pltpu.VMEM((512, PAIR), half),
            pltpu.VMEM((8, 512), jnp.float32),
            pltpu.VMEM((PAIR, 512), jnp.float32),
            pltpu.VMEM((512, PAIR), jnp.float32),
            pltpu.VMEM((512, PAIR), jnp.float32),
            *(pltpu.VMEM((rows, cols // SW, SW, width), half) for _ in range(5)),
            pltpu.VMEM((rows, cols // SW, SW, HEADS), jnp.float32),
            dma((6,)),
            dma((4, peers)), dma((4, peers)), dma((peers,)), dma((peers,)),
            dma((5,)), dma((5,)), dma((3, peers)), dma((3, peers)), dma((3,)), dma((3,)),
        ],
        compiler_params=pltpu.CompilerParams(
            collective_id=0, has_side_effects=True, vmem_limit_bytes=63 * 1024 * 1024
        ),
    )(
        view(queries), view(key_map), view(value_map), view(saved_output), view(output_grad),
        view(saved_logsum),
    )
    return tuple(values.astype(jnp.float32).reshape(rows, cols, width) for values in grads)


def local(mesh, *arrays):
    peers = mesh.shape["row"]
    if peers == 8 and mesh.shape["col"] == 2 and arrays[0].shape == (8, 16, HEADS * HD):
        return local_exchange(peers, *arrays)
    return local_general(*arrays)


def solution(mesh):
    in_specs = (
        P(("grp", "row"), "col", None),
        P(("grp", "row"), "col", None),
        P(("grp", "row"), "col", None),
        P(("grp", "row"), "col", None),
        P(("grp", "row"), "col", None),
        P(("grp", "row"), "col", None),
    )
    out_specs = (
        P(("grp", "row"), "col", None),
        P(("grp", "row"), "col", None),
        P(("grp", "row"), "col", None),
    )
    return jax.shard_map(functools.partial(local, mesh), mesh=mesh, in_specs=in_specs, out_specs=out_specs, check_vma=False)
```

```python
import functools
import math

import jax
import jax.numpy as jnp
from jax import lax
from jax.experimental import pallas as pl
from jax.experimental.pallas import tpu as pltpu
from jax.sharding import PartitionSpec as P

HEADS = 16
HD = 64
SW = 8


def attention_terms(
    stripe_query, stripe_key, stripe_value, stripe_grad, stripe_logsum, stripe_delta
):
    scale = 1.0 / math.sqrt(HD)
    scores = (
        jnp.einsum("gahe,gbhe->ghab", stripe_query, stripe_key, preferred_element_type=jnp.float32)
        * scale
    )
    probs = jnp.exp(scores - jnp.swapaxes(stripe_logsum, 1, 2)[..., None])
    grad_probs = jnp.einsum(
        "gahe,gbhe->ghab", stripe_grad, stripe_value, preferred_element_type=jnp.float32
    )
    grad_scores = (probs * (grad_probs - jnp.swapaxes(stripe_delta, 1, 2)[..., None])).astype(
        jnp.bfloat16
    )
    return (probs.astype(jnp.bfloat16), grad_scores)


def query_side(grad_scores, stripe_key):
    total = jnp.einsum(
        "ghab,gbhe->gahe", grad_scores, stripe_key, preferred_element_type=jnp.float32
    )
    return total * (1.0 / math.sqrt(HD))


def key_side(probs_half, grad_scores, stripe_query, stripe_grad):
    key_total = jnp.einsum(
        "ghab,gahe->gbhe", grad_scores, stripe_query, preferred_element_type=jnp.float32
    )
    value_total = jnp.einsum(
        "ghab,gahe->gbhe", probs_half, stripe_grad, preferred_element_type=jnp.float32
    )
    return (key_total * (1.0 / math.sqrt(HD)), value_total)


def in_blocks(step, carry, arrays, size):
    length = arrays[0].shape[0]

    def turn(index, total):
        parts = tuple((lax.dynamic_slice_in_dim(array, index * size, size, 0) for array in arrays))
        return step(total, parts)

    return lax.fori_loop(0, length // size, turn, carry)


def local_general(queries, key_map, value_map, saved_output, output_grad, saved_logsum):
    rows, cols, width = queries.shape
    half = HEADS // 2
    split = half * HD
    tail = (half, HD)
    block = 4 * rows
    products = output_grad.astype(jnp.float32) * saved_output.astype(jnp.float32)
    delta_all = jnp.sum(products.reshape(rows, cols, HEADS, HD), axis=3)

    def row_group(values, last):
        return values.reshape((rows // SW, SW * values.shape[1]) + last)

    def column_group(values, last):
        count = values.shape[0]
        shaped = values.reshape((count, cols // SW, SW) + last)
        return jnp.swapaxes(shaped, 0, 1).reshape((cols // SW, count * SW) + last)

    def column_back(values, count):
        shaped = values.reshape((cols // SW, count, SW, -1))
        return jnp.swapaxes(shaped, 0, 1).reshape(count, cols, -1)

    full_key, full_value = (
        lax.all_gather(key_map[:, :, :split], "col", axis=1, tiled=True),
        lax.all_gather(value_map[:, :, :split], "col", axis=1, tiled=True),
    )
    wide = full_key.shape[1]
    stripe_query = row_group(queries[:, :, :split], tail)
    stripe_grad = row_group(output_grad[:, :, :split], tail)
    stripe_logsum = row_group(saved_logsum[:, :, :half], (half,))
    stripe_delta = row_group(delta_all[:, :, :half], (half,))
    stripe_key = row_group(full_key, tail)
    stripe_value = row_group(full_value, tail)
    probs_half, grad_scores = attention_terms(
        stripe_query, stripe_key, stripe_value, stripe_grad, stripe_logsum, stripe_delta
    )
    row_query_grad = query_side(grad_scores, stripe_key).reshape(rows, cols, split)
    row_key_part, row_value_part = key_side(probs_half, grad_scores, stripe_query, stripe_grad)
    row_term = jnp.concatenate(
        (row_key_part.reshape(rows, wide, split), row_value_part.reshape(rows, wide, split)), axis=2
    )
    row_sums = lax.psum_scatter(row_term, "col", scatter_dimension=1, tiled=True)
    local_key = key_map[:, :, split:]
    local_value = value_map[:, :, split:]
    column_query = column_group(queries[:, :, split:], tail)
    column_grad = column_group(output_grad[:, :, split:], tail)
    column_logsum = column_group(saved_logsum[:, :, half:], (half,))
    column_delta = column_group(delta_all[:, :, half:], (half,))

    def query_step(total, pieces):
        grouped_key = column_group(pieces[0], tail)
        grouped_value = column_group(pieces[1], tail)
        weights, gradients = attention_terms(
            column_query, grouped_key, grouped_value, column_grad, column_logsum, column_delta
        )
        return total + query_side(gradients, grouped_key)

    empty_query = jnp.zeros(column_query.shape, jnp.float32)
    every_key, every_value = (
        lax.all_gather(local_key, "row", axis=0, tiled=True),
        lax.all_gather(local_value, "row", axis=0, tiled=True),
    )
    column_total = in_blocks(query_step, empty_query, (every_key, every_value), block)

    def key_step(pieces):
        count = pieces[0].shape[0]
        grouped_key = column_group(pieces[0], tail)
        grouped_value = column_group(pieces[1], tail)
        weights, gradients = attention_terms(
            column_query, grouped_key, grouped_value, column_grad, column_logsum, column_delta
        )
        key_part, value_part = key_side(weights, gradients, column_query, column_grad)
        return jnp.concatenate(
            (column_back(key_part, count), column_back(value_part, count)), axis=2
        )

    count = rows * lax.axis_size("row")
    stacked = lax.map(
        key_step,
        (
            every_key.reshape((count // block, block) + every_key.shape[1:]),
            every_value.reshape((count // block, block) + every_value.shape[1:]),
        ),
    )
    column_sums = lax.psum_scatter(
        stacked.reshape((count,) + stacked.shape[2:]), "row", scatter_dimension=0, tiled=True
    )
    column_key_grad = column_sums[:, :, :split]
    column_value_grad = column_sums[:, :, split:]
    column_query_grad = column_back(column_total, rows)
    query_grad = jnp.concatenate((row_query_grad, column_query_grad), axis=2)
    key_grad = jnp.concatenate((row_sums[:, :, :split], column_key_grad), axis=2)
    value_grad = jnp.concatenate((row_sums[:, :, split:], column_value_grad), axis=2)
    return (query_grad, key_grad, value_grad)


MESH = pl.DeviceIdType.MESH
NT = (((1,), (1,)), ((), ()))
TN = (((0,), (0,)), ((), ()))
PAIR = 2 * HD


def flat(values):
    return values.astype(jnp.float32).reshape((-1, values.shape[-1]))


def attend(count, block, q_s, k_s, v_s, g_s, rows, dq_t, dk_s, dv_s):
    scale = 1.0 / math.sqrt(HD)
    lane = lax.broadcasted_iota(jnp.int32, (block, PAIR), 1)
    masks = tuple(((lane // HD) == h).astype(jnp.float32).astype(jnp.bfloat16) for h in (0, 1))

    def step(j, carry):
        part = pl.ds(pl.multiple_of(j * block, block), block)
        q = q_s[0:count, :]
        g = g_s[0:count, :]
        keys = k_s[part, :]
        values = v_s[part, :]
        dk = []
        dv = []
        dq = None
        for h in (0, 1):
            key = keys * masks[h]
            value = values * masks[h]
            scores = lax.dot_general(key, q, NT, preferred_element_type=jnp.float32)
            probs = jnp.exp(scores * scale - rows[h : h + 1, 0:count])
            grad_probs = lax.dot_general(value, g, NT, preferred_element_type=jnp.float32)
            grad_scores = (probs * (grad_probs - rows[2 + h : 3 + h, 0:count])).astype(jnp.bfloat16)
            half = probs.astype(jnp.bfloat16)
            dv.append(jnp.dot(half, g, preferred_element_type=jnp.float32))
            dk.append(jnp.dot(grad_scores, q, preferred_element_type=jnp.float32))
            term = lax.dot_general(key, grad_scores, TN, preferred_element_type=jnp.float32)
            dq = term if dq is None else dq + term
        dk_s[part, :] = jnp.where(lane < HD, dk[0], dk[1]) * scale
        dv_s[part, :] = jnp.where(lane < HD, dv[0], dv[1])
        dq_t[:, 0:count] += dq
        return carry

    dq_t[:, 0:count] = jnp.zeros((PAIR, count), jnp.float32)
    lax.fori_loop(0, count // block, step, 0)
    return dq_t[:, 0:count].T * scale


def exchange_kernel(
    q_hbm, k_hbm, v_hbm, o_hbm, g_hbm, l_hbm,
    dq_ref, dk_ref, dv_ref,
    col_in, col_aux, row_in, row_aux, aux_row, aux_col, col_out, row_out,
    q_s, k_s, v_s, g_s, rows_s, dq_t, dk_s, dv_s,
    q_ref, k_ref, v_ref, o_ref, g_ref, l_ref, row_own, keep_sem, in_sem,
    cs_sem, cr_sem, as_sem, ar_sem, rs_sem, rr_sem, os_sem, or_sem, ps_sem, pr_sem,
):
    me = lax.axis_index("row")
    core = lax.axis_index("col")
    peers = lax.axis_size("row")
    other = 1 - core
    split = (HEADS // 2) * HD
    pair = me // 2
    stripe = me % 2
    ins = (q_ref, k_ref, v_ref, g_ref)
    outs = (dq_ref, dk_ref, dv_ref)
    sources = (q_hbm, k_hbm, v_hbm, g_hbm)
    loads = [
        pltpu.make_async_copy(source, target, in_sem.at[n])
        for n, (source, target) in enumerate(
            (
                (g_hbm, g_ref), (o_hbm, o_ref), (l_hbm, l_ref),
                (q_hbm, q_ref), (k_hbm, k_ref), (v_hbm, v_ref),
            )
        )
    ]
    for load in loads:
        load.start()

    barrier = pltpu.get_barrier_semaphore()
    for step in range(1, peers):
        pl.semaphore_signal(
            barrier, inc=1, device_id={"row": lax.rem(me + step, peers)}, device_id_type=MESH
        )
    pl.semaphore_signal(barrier, inc=1, device_id={"col": other}, device_id_type=MESH)
    pl.semaphore_wait(barrier, peers)

    def col_lanes(index):
        return pl.ds(pl.multiple_of(split + PAIR * index, PAIR), PAIR)

    def core_lanes(index):
        return pl.ds(pl.multiple_of(2 * PAIR * index, 2 * PAIR), 2 * PAIR)

    def eight(index):
        return pl.ds(pl.multiple_of(index * 8, 8), 8)

    def row_copy(a):
        return pltpu.make_async_remote_copy(
            src_ref=sources[a].at[:, :, :, core_lanes(other)],
            dst_ref=row_in.at[a],
            send_sem=rs_sem.at[a], recv_sem=rr_sem.at[a],
            device_id={"col": other}, device_id_type=MESH,
        )

    def col_copy(a, target, source):
        return pltpu.make_async_remote_copy(
            src_ref=sources[a].at[:, target % 2, :, col_lanes(target // 2)],
            dst_ref=col_in.at[a, eight(source)],
            send_sem=cs_sem.at[a, target], recv_sem=cr_sem.at[a, source],
            device_id={"row": target}, device_id_type=MESH,
        )

    def aux_copy(target, source):
        return pltpu.make_async_remote_copy(
            src_ref=aux_col.at[target // 2],
            dst_ref=col_aux.at[source],
            send_sem=as_sem.at[target], recv_sem=ar_sem.at[source],
            device_id={"row": target}, device_id_type=MESH,
        )

    def back_copy(a, target, owner):
        return pltpu.make_async_remote_copy(
            src_ref=col_out.at[a, eight(target)],
            dst_ref=outs[a].at[:, owner % 2, :, col_lanes(owner // 2)],
            send_sem=os_sem.at[a, target], recv_sem=or_sem.at[a, owner],
            device_id={"row": target}, device_id_type=MESH,
        )

    def row_back(a, owner):
        return pltpu.make_async_remote_copy(
            src_ref=row_out.at[a],
            dst_ref=outs[a].at[:, :, :, core_lanes(owner)],
            send_sem=ps_sem.at[a], recv_sem=pr_sem.at[a],
            device_id={"col": other}, device_id_type=MESH,
        )

    def row_keep(a):
        return pltpu.make_async_copy(
            row_own.at[a], outs[a].at[:, :, :, core_lanes(core)], keep_sem.at[a]
        )

    def col_keep(a):
        return pltpu.make_async_copy(
            col_out.at[a, eight(me)], outs[a].at[:, stripe, :, col_lanes(pair)], keep_sem.at[3 + a]
        )

    def row_aux_copy():
        return pltpu.make_async_remote_copy(
            src_ref=aux_row.at[pl.ds(2 * other, 2)],
            dst_ref=row_aux,
            send_sem=rs_sem.at[4], recv_sem=rr_sem.at[4],
            device_id={"col": other}, device_id_type=MESH,
        )

    for a in range(4):
        row_copy(a).start()

    def partner(step):
        flip = jnp.where(step < 5, step + 3, step - 4)
        return (me // 4 + flip // 4) % 2 * 4 + (me // 2 + flip // 2) % 2 * 2 + (me + flip) % 2

    def send(step, carry):
        target = partner(step)
        for a in range(4):
            col_copy(a, target, me).start()
        return carry

    lax.fori_loop(1, peers, send, 0)

    for load in loads[:3]:
        load.wait()
    which = lax.broadcasted_iota(jnp.int32, (8, PAIR), 0)
    lane = lax.broadcasted_iota(jnp.int32, (8, PAIR), 1)
    pick = (which == 2 + lane // HD).astype(jnp.float32)
    which_l = lax.broadcasted_iota(jnp.int32, (8, HEADS), 0)
    lane_l = lax.broadcasted_iota(jnp.int32, (8, HEADS), 1)
    sums_row = flat(l_ref[...])
    sums_col = jnp.concatenate((flat(l_ref[:, 0]), flat(l_ref[:, 1])), axis=0)
    exact = functools.partial(
        lax.dot_general, dimension_numbers=NT, precision=lax.Precision.HIGHEST,
        preferred_element_type=jnp.float32,
    )
    for t in range(HEADS // 2):
        part = slice(t * PAIR, (t + 1) * PAIR)
        choose = ((lane_l - 2 * t == which_l) & (which_l < 2)).astype(jnp.float32)
        if t < HEADS // 4:
            products = flat(g_ref[:, :, :, part]) * flat(o_ref[:, :, :, part])
            aux_row[t] = exact(pick, products) + exact(choose, sums_row)
        else:
            products = jnp.concatenate(
                tuple(flat(g_ref[:, s, :, part]) * flat(o_ref[:, s, :, part]) for s in (0, 1)),
                axis=0,
            )
            aux_col[t - HEADS // 4] = exact(pick, products) + exact(choose, sums_col)

    row_aux_copy().start()

    def send_aux(step, carry):
        aux_copy(partner(step), me).start()
        return carry

    lax.fori_loop(1, peers, send_aux, 0)
    for load in loads[3:]:
        load.wait()
    for a in range(4):
        col_in[a, eight(me)] = ins[a][:, stripe, :, col_lanes(pair)]
    col_aux[me] = aux_col[pair]

    for a in range(4):
        row_copy(a).wait_recv()
    row_aux_copy().wait_recv()
    scratch = (q_s, k_s, v_s, g_s)
    for u in (0, 1):
        part = slice(u * PAIR, (u + 1) * PAIR)
        mine = pl.ds(pl.multiple_of(2 * PAIR * core + u * PAIR, PAIR), PAIR)
        for a in range(4):
            scratch[a][0:128, :] = flat(ins[a][:, :, :, mine]).astype(jnp.bfloat16)
            scratch[a][128:256, :] = flat(row_in[a, :, :, :, part]).astype(jnp.bfloat16)
        rows_s[:, 0:128] = aux_row[2 * core + u]
        rows_s[:, 128:256] = row_aux[u]
        dq = attend(256, 256, q_s, k_s, v_s, g_s, rows_s, dq_t, dk_s, dv_s)
        for a, grads in enumerate((dq, dk_s[0:256, :], dv_s[0:256, :])):
            shaped = grads.reshape((2, 8, 2, 8, PAIR)).astype(jnp.bfloat16)
            row_own[a, :, :, :, part] = shaped[0]
            row_out[a, :, :, :, part] = shaped[1]
    for a in range(3):
        row_back(a, core).start()
        row_keep(a).start()

    def arrive(step, carry):
        source = partner(step)
        for a in range(4):
            col_copy(a, source, source).wait_recv()
        aux_copy(source, source).wait_recv()
        return carry

    lax.fori_loop(1, peers, arrive, 0)
    for a in range(4):
        scratch[a][...] = flat(col_in[a]).astype(jnp.bfloat16)
    low = lane < HD
    for k in range(4):
        first = col_aux[2 * k]
        second = col_aux[2 * k + 1]
        even = jnp.where(low, first, pltpu.roll(second, HD, 1))
        odd = jnp.where(low, pltpu.roll(first, HD, 1), second)
        rows_s[:, k * PAIR : (k + 1) * PAIR] = jnp.where(stripe == 0, even, odd)
    dq = attend(512, 256, q_s, k_s, v_s, g_s, rows_s, dq_t, dk_s, dv_s)
    for a, grads in enumerate((dq, dk_s[...], dv_s[...])):
        col_out[a] = grads.reshape((64, 8, PAIR)).astype(jnp.bfloat16)

    def give(step, carry):
        target = partner(step)
        for a in range(3):
            back_copy(a, target, me).start()
        return carry

    lax.fori_loop(1, peers, give, 0)
    for a in range(3):
        col_keep(a).start()

    def finish(step, carry):
        target = partner(step)
        for a in range(3):
            back_copy(a, target, target).wait_recv()
        for a in range(3):
            back_copy(a, target, me).wait_send()
        for a in range(4):
            col_copy(a, target, me).wait_send()
        aux_copy(target, me).wait_send()
        return carry

    for a in range(4):
        row_copy(a).wait_send()
    row_aux_copy().wait_send()
    for a in range(3):
        row_back(a, core).wait()
        row_keep(a).wait()
        col_keep(a).wait()
    lax.fori_loop(1, peers, finish, 0)


def widen_kernel(*refs):
    for narrow, wide in zip(refs[:3], refs[3:]):
        wide[...] = narrow[...].astype(jnp.float32).reshape(wide.shape)


def local_exchange(peers, queries, key_map, value_map, saved_output, output_grad, saved_logsum):
    rows, cols, width = queries.shape

    def view(values):
        return values.reshape((rows, cols // SW, SW, values.shape[-1]))

    half = jnp.bfloat16
    hbm = pl.BlockSpec(memory_space=pltpu.HBM)
    dma = pltpu.SemaphoreType.DMA
    grads = pl.pallas_call(
        exchange_kernel,
        out_shape=(jax.ShapeDtypeStruct((rows, cols // SW, SW, width), half),) * 3,
        in_specs=[hbm] * 6,
        out_specs=(hbm,) * 3,
        scratch_shapes=[
            pltpu.VMEM((4, 8 * peers, SW, PAIR), half),
            pltpu.VMEM((peers, 8, PAIR), jnp.float32),
            pltpu.VMEM((4, rows, cols // SW, SW, 2 * PAIR), half),
            pltpu.VMEM((2, 8, PAIR), jnp.float32),
            pltpu.VMEM((4, 8, PAIR), jnp.float32),
            pltpu.VMEM((4, 8, PAIR), jnp.float32),
            pltpu.VMEM((3, 8 * peers, SW, PAIR), half),
            pltpu.VMEM((3, rows, cols // SW, SW, 2 * PAIR), half),
            pltpu.VMEM((512, PAIR), half),
            pltpu.VMEM((512, PAIR), half),
            pltpu.VMEM((512, PAIR), half),
            pltpu.VMEM((512, PAIR), half),
            pltpu.VMEM((8, 512), jnp.float32),
            pltpu.VMEM((PAIR, 512), jnp.float32),
            pltpu.VMEM((512, PAIR), jnp.float32),
            pltpu.VMEM((512, PAIR), jnp.float32),
            *(pltpu.VMEM((rows, cols // SW, SW, width), half) for _ in range(5)),
            pltpu.VMEM((rows, cols // SW, SW, HEADS), jnp.float32),
            pltpu.VMEM((3, rows, cols // SW, SW, 2 * PAIR), half),
            dma((6,)),
            dma((6,)),
            dma((4, peers)), dma((4, peers)), dma((peers,)), dma((peers,)),
            dma((5,)), dma((5,)), dma((3, peers)), dma((3, peers)), dma((3,)), dma((3,)),
        ],
        compiler_params=pltpu.CompilerParams(
            collective_id=0, has_side_effects=True, vmem_limit_bytes=63 * 1024 * 1024
        ),
    )(
        view(queries), view(key_map), view(value_map), view(saved_output), view(output_grad),
        view(saved_logsum),
    )
    steps = 4
    narrow = pl.BlockSpec((rows // steps, cols // SW, SW, width), lambda i: (i, 0, 0, 0))
    wide = pl.BlockSpec((rows // steps, cols, width), lambda i: (i, 0, 0))
    return tuple(
        pl.pallas_call(
            widen_kernel,
            grid=(steps,),
            out_shape=(jax.ShapeDtypeStruct((rows, cols, width), jnp.float32),) * 3,
            in_specs=[narrow] * 3,
            out_specs=(wide,) * 3,
            compiler_params=pltpu.CompilerParams(vmem_limit_bytes=63 * 1024 * 1024),
        )(*grads)
    )


def local(mesh, *arrays):
    peers = mesh.shape["row"]
    if peers == 8 and mesh.shape["col"] == 2 and arrays[0].shape == (8, 16, HEADS * HD):
        return local_exchange(peers, *arrays)
    return local_general(*arrays)


def solution(mesh):
    in_specs = (
        P(("grp", "row"), "col", None),
        P(("grp", "row"), "col", None),
        P(("grp", "row"), "col", None),
        P(("grp", "row"), "col", None),
        P(("grp", "row"), "col", None),
        P(("grp", "row"), "col", None),
    )
    out_specs = (
        P(("grp", "row"), "col", None),
        P(("grp", "row"), "col", None),
        P(("grp", "row"), "col", None),
    )
    return jax.shard_map(functools.partial(local, mesh), mesh=mesh, in_specs=in_specs, out_specs=out_specs, check_vma=False)
```

```python
import functools
import math

import jax
import jax.numpy as jnp
from jax import lax
from jax.experimental import pallas as pl
from jax.experimental.pallas import tpu as pltpu
from jax.sharding import PartitionSpec as P

HEADS = 16
HD = 64
SW = 8


def attention_terms(
    stripe_query, stripe_key, stripe_value, stripe_grad, stripe_logsum, stripe_delta
):
    scale = 1.0 / math.sqrt(HD)
    scores = (
        jnp.einsum("gahe,gbhe->ghab", stripe_query, stripe_key, preferred_element_type=jnp.float32)
        * scale
    )
    probs = jnp.exp(scores - jnp.swapaxes(stripe_logsum, 1, 2)[..., None])
    grad_probs = jnp.einsum(
        "gahe,gbhe->ghab", stripe_grad, stripe_value, preferred_element_type=jnp.float32
    )
    grad_scores = (probs * (grad_probs - jnp.swapaxes(stripe_delta, 1, 2)[..., None])).astype(
        jnp.bfloat16
    )
    return (probs.astype(jnp.bfloat16), grad_scores)


def query_side(grad_scores, stripe_key):
    total = jnp.einsum(
        "ghab,gbhe->gahe", grad_scores, stripe_key, preferred_element_type=jnp.float32
    )
    return total * (1.0 / math.sqrt(HD))


def key_side(probs_half, grad_scores, stripe_query, stripe_grad):
    key_total = jnp.einsum(
        "ghab,gahe->gbhe", grad_scores, stripe_query, preferred_element_type=jnp.float32
    )
    value_total = jnp.einsum(
        "ghab,gahe->gbhe", probs_half, stripe_grad, preferred_element_type=jnp.float32
    )
    return (key_total * (1.0 / math.sqrt(HD)), value_total)


def in_blocks(step, carry, arrays, size):
    length = arrays[0].shape[0]

    def turn(index, total):
        parts = tuple((lax.dynamic_slice_in_dim(array, index * size, size, 0) for array in arrays))
        return step(total, parts)

    return lax.fori_loop(0, length // size, turn, carry)


def local_general(queries, key_map, value_map, saved_output, output_grad, saved_logsum):
    rows, cols, width = queries.shape
    half = HEADS // 2
    split = half * HD
    tail = (half, HD)
    block = 4 * rows
    products = output_grad.astype(jnp.float32) * saved_output.astype(jnp.float32)
    delta_all = jnp.sum(products.reshape(rows, cols, HEADS, HD), axis=3)

    def row_group(values, last):
        return values.reshape((rows // SW, SW * values.shape[1]) + last)

    def column_group(values, last):
        count = values.shape[0]
        shaped = values.reshape((count, cols // SW, SW) + last)
        return jnp.swapaxes(shaped, 0, 1).reshape((cols // SW, count * SW) + last)

    def column_back(values, count):
        shaped = values.reshape((cols // SW, count, SW, -1))
        return jnp.swapaxes(shaped, 0, 1).reshape(count, cols, -1)

    full_key, full_value = (
        lax.all_gather(key_map[:, :, :split], "col", axis=1, tiled=True),
        lax.all_gather(value_map[:, :, :split], "col", axis=1, tiled=True),
    )
    wide = full_key.shape[1]
    stripe_query = row_group(queries[:, :, :split], tail)
    stripe_grad = row_group(output_grad[:, :, :split], tail)
    stripe_logsum = row_group(saved_logsum[:, :, :half], (half,))
    stripe_delta = row_group(delta_all[:, :, :half], (half,))
    stripe_key = row_group(full_key, tail)
    stripe_value = row_group(full_value, tail)
    probs_half, grad_scores = attention_terms(
        stripe_query, stripe_key, stripe_value, stripe_grad, stripe_logsum, stripe_delta
    )
    row_query_grad = query_side(grad_scores, stripe_key).reshape(rows, cols, split)
    row_key_part, row_value_part = key_side(probs_half, grad_scores, stripe_query, stripe_grad)
    row_term = jnp.concatenate(
        (row_key_part.reshape(rows, wide, split), row_value_part.reshape(rows, wide, split)), axis=2
    )
    row_sums = lax.psum_scatter(row_term, "col", scatter_dimension=1, tiled=True)
    local_key = key_map[:, :, split:]
    local_value = value_map[:, :, split:]
    column_query = column_group(queries[:, :, split:], tail)
    column_grad = column_group(output_grad[:, :, split:], tail)
    column_logsum = column_group(saved_logsum[:, :, half:], (half,))
    column_delta = column_group(delta_all[:, :, half:], (half,))

    def query_step(total, pieces):
        grouped_key = column_group(pieces[0], tail)
        grouped_value = column_group(pieces[1], tail)
        weights, gradients = attention_terms(
            column_query, grouped_key, grouped_value, column_grad, column_logsum, column_delta
        )
        return total + query_side(gradients, grouped_key)

    empty_query = jnp.zeros(column_query.shape, jnp.float32)
    every_key, every_value = (
        lax.all_gather(local_key, "row", axis=0, tiled=True),
        lax.all_gather(local_value, "row", axis=0, tiled=True),
    )
    column_total = in_blocks(query_step, empty_query, (every_key, every_value), block)

    def key_step(pieces):
        count = pieces[0].shape[0]
        grouped_key = column_group(pieces[0], tail)
        grouped_value = column_group(pieces[1], tail)
        weights, gradients = attention_terms(
            column_query, grouped_key, grouped_value, column_grad, column_logsum, column_delta
        )
        key_part, value_part = key_side(weights, gradients, column_query, column_grad)
        return jnp.concatenate(
            (column_back(key_part, count), column_back(value_part, count)), axis=2
        )

    count = rows * lax.axis_size("row")
    stacked = lax.map(
        key_step,
        (
            every_key.reshape((count // block, block) + every_key.shape[1:]),
            every_value.reshape((count // block, block) + every_value.shape[1:]),
        ),
    )
    column_sums = lax.psum_scatter(
        stacked.reshape((count,) + stacked.shape[2:]), "row", scatter_dimension=0, tiled=True
    )
    column_key_grad = column_sums[:, :, :split]
    column_value_grad = column_sums[:, :, split:]
    column_query_grad = column_back(column_total, rows)
    query_grad = jnp.concatenate((row_query_grad, column_query_grad), axis=2)
    key_grad = jnp.concatenate((row_sums[:, :, :split], column_key_grad), axis=2)
    value_grad = jnp.concatenate((row_sums[:, :, split:], column_value_grad), axis=2)
    return (query_grad, key_grad, value_grad)


MESH = pl.DeviceIdType.MESH
NT = (((1,), (1,)), ((), ()))
TN = (((0,), (0,)), ((), ()))
PAIR = 2 * HD


def flat(values):
    return values.astype(jnp.float32).reshape((-1, values.shape[-1]))


def attend(count, block, q_s, k_s, v_s, g_s, rows, dq_t, dk_s, dv_s):
    scale = 1.0 / math.sqrt(HD)
    lane = lax.broadcasted_iota(jnp.int32, (block, PAIR), 1)
    masks = tuple(((lane // HD) == h).astype(jnp.float32).astype(jnp.bfloat16) for h in (0, 1))

    def step(j, carry):
        part = pl.ds(pl.multiple_of(j * block, block), block)
        q = q_s[0:count, :]
        g = g_s[0:count, :]
        keys = k_s[part, :]
        values = v_s[part, :]
        dk = []
        dv = []
        dq = None
        for h in (0, 1):
            key = keys * masks[h]
            value = values * masks[h]
            scores = lax.dot_general(key, q, NT, preferred_element_type=jnp.float32)
            probs = jnp.exp(scores * scale - rows[h : h + 1, 0:count])
            grad_probs = lax.dot_general(value, g, NT, preferred_element_type=jnp.float32)
            grad_scores = (probs * (grad_probs - rows[2 + h : 3 + h, 0:count])).astype(jnp.bfloat16)
            half = probs.astype(jnp.bfloat16)
            dv.append(jnp.dot(half, g, preferred_element_type=jnp.float32))
            dk.append(jnp.dot(grad_scores, q, preferred_element_type=jnp.float32))
            term = lax.dot_general(key, grad_scores, TN, preferred_element_type=jnp.float32)
            dq = term if dq is None else dq + term
        dk_s[part, :] = jnp.where(lane < HD, dk[0], dk[1]) * scale
        dv_s[part, :] = jnp.where(lane < HD, dv[0], dv[1])
        dq_t[:, 0:count] += dq
        return carry

    dq_t[:, 0:count] = jnp.zeros((PAIR, count), jnp.float32)
    lax.fori_loop(0, count // block, step, 0)
    return dq_t[:, 0:count].T * scale


def exchange_kernel(
    q_hbm, k_hbm, v_hbm, o_hbm, g_hbm, l_hbm,
    dq_ref, dk_ref, dv_ref,
    col_in, col_aux, row_in, row_aux, aux_row, aux_col, col_out, row_out,
    q_s, k_s, v_s, g_s, rows_s, dq_t, dk_s, dv_s,
    q_ref, k_ref, v_ref, o_ref, g_ref, l_ref, row_own, keep_sem, in_sem,
    cs_sem, cr_sem, as_sem, ar_sem, rs_sem, rr_sem, os_sem, or_sem, ps_sem, pr_sem,
):
    me = lax.axis_index("row")
    core = lax.axis_index("col")
    peers = lax.axis_size("row")
    other = 1 - core
    split = (HEADS // 2) * HD
    pair = me // 2
    stripe = me % 2
    ins = (q_ref, k_ref, v_ref, g_ref)
    outs = (dq_ref, dk_ref, dv_ref)
    sources = (q_hbm, k_hbm, v_hbm, g_hbm)
    loads = [
        pltpu.make_async_copy(source, target, in_sem.at[n])
        for n, (source, target) in enumerate(
            (
                (g_hbm, g_ref), (o_hbm, o_ref), (l_hbm, l_ref),
                (q_hbm, q_ref), (k_hbm, k_ref), (v_hbm, v_ref),
            )
        )
    ]
    for load in loads:
        load.start()

    barrier = pltpu.get_barrier_semaphore()
    for step in range(1, peers):
        pl.semaphore_signal(
            barrier, inc=1, device_id={"row": lax.rem(me + step, peers)}, device_id_type=MESH
        )
    pl.semaphore_signal(barrier, inc=1, device_id={"col": other}, device_id_type=MESH)
    pl.semaphore_wait(barrier, peers)

    def col_lanes(index):
        return pl.ds(pl.multiple_of(split + PAIR * index, PAIR), PAIR)

    def core_lanes(index):
        return pl.ds(pl.multiple_of(2 * PAIR * index, 2 * PAIR), 2 * PAIR)

    def eight(index):
        return pl.ds(pl.multiple_of(index * 8, 8), 8)

    def row_copy(a):
        return pltpu.make_async_remote_copy(
            src_ref=sources[a].at[:, :, :, core_lanes(other)],
            dst_ref=row_in.at[a],
            send_sem=rs_sem.at[a], recv_sem=rr_sem.at[a],
            device_id={"col": other}, device_id_type=MESH,
        )

    def col_copy(a, target, source):
        return pltpu.make_async_remote_copy(
            src_ref=sources[a].at[:, target % 2, :, col_lanes(target // 2)],
            dst_ref=col_in.at[a, eight(source)],
            send_sem=cs_sem.at[a, target], recv_sem=cr_sem.at[a, source],
            device_id={"row": target}, device_id_type=MESH,
        )

    def aux_copy(target, source):
        return pltpu.make_async_remote_copy(
            src_ref=aux_col.at[target // 2],
            dst_ref=col_aux.at[source],
            send_sem=as_sem.at[target], recv_sem=ar_sem.at[source],
            device_id={"row": target}, device_id_type=MESH,
        )

    def back_copy(a, target, owner):
        return pltpu.make_async_remote_copy(
            src_ref=col_out.at[a, eight(target)],
            dst_ref=outs[a].at[:, owner % 2, :, col_lanes(owner // 2)],
            send_sem=os_sem.at[a, target], recv_sem=or_sem.at[a, owner],
            device_id={"row": target}, device_id_type=MESH,
        )

    def row_back(a, owner):
        return pltpu.make_async_remote_copy(
            src_ref=row_out.at[a],
            dst_ref=outs[a].at[:, :, :, core_lanes(owner)],
            send_sem=ps_sem.at[a], recv_sem=pr_sem.at[a],
            device_id={"col": other}, device_id_type=MESH,
        )

    def row_keep(a):
        return pltpu.make_async_copy(
            row_own.at[a], outs[a].at[:, :, :, core_lanes(core)], keep_sem.at[a]
        )

    def col_keep(a):
        return pltpu.make_async_copy(
            col_out.at[a, eight(me)], outs[a].at[:, stripe, :, col_lanes(pair)], keep_sem.at[3 + a]
        )

    def row_aux_copy():
        return pltpu.make_async_remote_copy(
            src_ref=aux_row.at[pl.ds(2 * other, 2)],
            dst_ref=row_aux,
            send_sem=rs_sem.at[4], recv_sem=rr_sem.at[4],
            device_id={"col": other}, device_id_type=MESH,
        )

    for a in range(4):
        row_copy(a).start()

    def partner(step):
        flip = jnp.where(step < 5, step + 3, step - 4)
        return (me // 4 + flip // 4) % 2 * 4 + (me // 2 + flip // 2) % 2 * 2 + (me + flip) % 2

    def send(step, carry):
        target = partner(step)
        for a in range(4):
            col_copy(a, target, me).start()
        return carry

    lax.fori_loop(1, peers, send, 0)

    for load in loads[:3]:
        load.wait()
    which = lax.broadcasted_iota(jnp.int32, (8, PAIR), 0)
    lane = lax.broadcasted_iota(jnp.int32, (8, PAIR), 1)
    pick = (which == 2 + lane // HD).astype(jnp.float32)
    which_l = lax.broadcasted_iota(jnp.int32, (8, HEADS), 0)
    lane_l = lax.broadcasted_iota(jnp.int32, (8, HEADS), 1)
    sums_row = flat(l_ref[...])
    sums_col = jnp.concatenate((flat(l_ref[:, 0]), flat(l_ref[:, 1])), axis=0)
    exact = functools.partial(
        lax.dot_general, dimension_numbers=NT, precision=lax.Precision.HIGHEST,
        preferred_element_type=jnp.float32,
    )
    for t in range(HEADS // 2):
        part = slice(t * PAIR, (t + 1) * PAIR)
        choose = ((lane_l - 2 * t == which_l) & (which_l < 2)).astype(jnp.float32)
        if t < HEADS // 4:
            products = flat(g_ref[:, :, :, part]) * flat(o_ref[:, :, :, part])
            aux_row[t] = exact(pick, products) + exact(choose, sums_row)
        else:
            products = jnp.concatenate(
                tuple(flat(g_ref[:, s, :, part]) * flat(o_ref[:, s, :, part]) for s in (0, 1)),
                axis=0,
            )
            aux_col[t - HEADS // 4] = exact(pick, products) + exact(choose, sums_col)

    row_aux_copy().start()

    def send_aux(step, carry):
        aux_copy(partner(step), me).start()
        return carry

    lax.fori_loop(1, peers, send_aux, 0)
    for load in loads[3:]:
        load.wait()
    for a in range(4):
        col_in[a, eight(me)] = ins[a][:, stripe, :, col_lanes(pair)]
    col_aux[me] = aux_col[pair]

    for a in range(4):
        row_copy(a).wait_recv()
    row_aux_copy().wait_recv()
    scratch = (q_s, k_s, v_s, g_s)
    for u in (0, 1):
        part = slice(u * PAIR, (u + 1) * PAIR)
        mine = pl.ds(pl.multiple_of(2 * PAIR * core + u * PAIR, PAIR), PAIR)
        for a in range(4):
            scratch[a][0:128, :] = flat(ins[a][:, :, :, mine]).astype(jnp.bfloat16)
            scratch[a][128:256, :] = flat(row_in[a, :, :, :, part]).astype(jnp.bfloat16)
        rows_s[:, 0:128] = aux_row[2 * core + u]
        rows_s[:, 128:256] = row_aux[u]
        dq = attend(256, 256, q_s, k_s, v_s, g_s, rows_s, dq_t, dk_s, dv_s)
        for a, grads in enumerate((dq, dk_s[0:256, :], dv_s[0:256, :])):
            shaped = grads.reshape((2, 8, 2, 8, PAIR)).astype(jnp.bfloat16)
            row_own[a, :, :, :, part] = shaped[0]
            row_out[a, :, :, :, part] = shaped[1]
    for a in range(3):
        row_back(a, core).start()
        row_keep(a).start()

    def arrive(step, carry):
        source = partner(step)
        for a in range(4):
            col_copy(a, source, source).wait_recv()
        aux_copy(source, source).wait_recv()
        return carry

    lax.fori_loop(1, peers, arrive, 0)
    for a in range(4):
        scratch[a][...] = flat(col_in[a]).astype(jnp.bfloat16)
    low = lane < HD
    for k in range(4):
        first = col_aux[2 * k]
        second = col_aux[2 * k + 1]
        even = jnp.where(low, first, pltpu.roll(second, HD, 1))
        odd = jnp.where(low, pltpu.roll(first, HD, 1), second)
        rows_s[:, k * PAIR : (k + 1) * PAIR] = jnp.where(stripe == 0, even, odd)
    dq = attend(512, 256, q_s, k_s, v_s, g_s, rows_s, dq_t, dk_s, dv_s)
    for a, grads in enumerate((dq, dk_s[...], dv_s[...])):
        col_out[a] = grads.reshape((64, 8, PAIR)).astype(jnp.bfloat16)

    def give(step, carry):
        target = partner(step)
        for a in range(3):
            back_copy(a, target, me).start()
        return carry

    lax.fori_loop(1, peers, give, 0)
    for a in range(3):
        col_keep(a).start()

    def finish(step, carry):
        target = partner(step)
        for a in range(3):
            back_copy(a, target, target).wait_recv()
        for a in range(3):
            back_copy(a, target, me).wait_send()
        for a in range(4):
            col_copy(a, target, me).wait_send()
        aux_copy(target, me).wait_send()
        return carry

    for a in range(4):
        row_copy(a).wait_send()
    row_aux_copy().wait_send()
    for a in range(3):
        row_back(a, core).wait()
        row_keep(a).wait()
        col_keep(a).wait()
    lax.fori_loop(1, peers, finish, 0)


def local_exchange(peers, queries, key_map, value_map, saved_output, output_grad, saved_logsum):
    rows, cols, width = queries.shape

    def view(values):
        return values.reshape((rows, cols // SW, SW, values.shape[-1]))

    half = jnp.bfloat16
    hbm = pl.BlockSpec(memory_space=pltpu.HBM)
    dma = pltpu.SemaphoreType.DMA
    grads = pl.pallas_call(
        exchange_kernel,
        out_shape=(pltpu.VMEM((rows, cols // SW, SW, width), half),) * 3,
        in_specs=[hbm] * 6,
        out_specs=(pl.BlockSpec(memory_space=pltpu.VMEM),) * 3,
        scratch_shapes=[
            pltpu.VMEM((4, 8 * peers, SW, PAIR), half),
            pltpu.VMEM((peers, 8, PAIR), jnp.float32),
            pltpu.VMEM((4, rows, cols // SW, SW, 2 * PAIR), half),
            pltpu.VMEM((2, 8, PAIR), jnp.float32),
            pltpu.VMEM((4, 8, PAIR), jnp.float32),
            pltpu.VMEM((4, 8, PAIR), jnp.float32),
            pltpu.VMEM((3, 8 * peers, SW, PAIR), half),
            pltpu.VMEM((3, rows, cols // SW, SW, 2 * PAIR), half),
            pltpu.VMEM((512, PAIR), half),
            pltpu.VMEM((512, PAIR), half),
            pltpu.VMEM((512, PAIR), half),
            pltpu.VMEM((512, PAIR), half),
            pltpu.VMEM((8, 512), jnp.float32),
            pltpu.VMEM((PAIR, 512), jnp.float32),
            pltpu.VMEM((512, PAIR), jnp.float32),
            pltpu.VMEM((512, PAIR), jnp.float32),
            *(pltpu.VMEM((rows, cols // SW, SW, width), half) for _ in range(5)),
            pltpu.VMEM((rows, cols // SW, SW, HEADS), jnp.float32),
            pltpu.VMEM((3, rows, cols // SW, SW, 2 * PAIR), half),
            dma((6,)),
            dma((6,)),
            dma((4, peers)), dma((4, peers)), dma((peers,)), dma((peers,)),
            dma((5,)), dma((5,)), dma((3, peers)), dma((3, peers)), dma((3,)), dma((3,)),
        ],
        compiler_params=pltpu.CompilerParams(
            collective_id=0, has_side_effects=True, vmem_limit_bytes=61 * 1024 * 1024
        ),
    )(
        view(queries), view(key_map), view(value_map), view(saved_output), view(output_grad),
        view(saved_logsum),
    )
    return tuple(values.astype(jnp.float32).reshape(rows, cols, width) for values in grads)


def local(mesh, *arrays):
    peers = mesh.shape["row"]
    if peers == 8 and mesh.shape["col"] == 2 and arrays[0].shape == (8, 16, HEADS * HD):
        return local_exchange(peers, *arrays)
    return local_general(*arrays)


def solution(mesh):
    in_specs = (
        P(("grp", "row"), "col", None),
        P(("grp", "row"), "col", None),
        P(("grp", "row"), "col", None),
        P(("grp", "row"), "col", None),
        P(("grp", "row"), "col", None),
        P(("grp", "row"), "col", None),
    )
    out_specs = (
        P(("grp", "row"), "col", None),
        P(("grp", "row"), "col", None),
        P(("grp", "row"), "col", None),
    )
    return jax.shard_map(functools.partial(local, mesh), mesh=mesh, in_specs=in_specs, out_specs=out_specs, check_vma=False)
```

```python
import functools
import math

import jax
import jax.numpy as jnp
from jax import lax
from jax.experimental import pallas as pl
from jax.experimental.pallas import tpu as pltpu
from jax.sharding import PartitionSpec as P

HEADS = 16
HD = 64
SW = 8


def attention_terms(
    stripe_query, stripe_key, stripe_value, stripe_grad, stripe_logsum, stripe_delta
):
    scale = 1.0 / math.sqrt(HD)
    scores = (
        jnp.einsum("gahe,gbhe->ghab", stripe_query, stripe_key, preferred_element_type=jnp.float32)
        * scale
    )
    probs = jnp.exp(scores - jnp.swapaxes(stripe_logsum, 1, 2)[..., None])
    grad_probs = jnp.einsum(
        "gahe,gbhe->ghab", stripe_grad, stripe_value, preferred_element_type=jnp.float32
    )
    grad_scores = (probs * (grad_probs - jnp.swapaxes(stripe_delta, 1, 2)[..., None])).astype(
        jnp.bfloat16
    )
    return (probs.astype(jnp.bfloat16), grad_scores)


def query_side(grad_scores, stripe_key):
    total = jnp.einsum(
        "ghab,gbhe->gahe", grad_scores, stripe_key, preferred_element_type=jnp.float32
    )
    return total * (1.0 / math.sqrt(HD))


def key_side(probs_half, grad_scores, stripe_query, stripe_grad):
    key_total = jnp.einsum(
        "ghab,gahe->gbhe", grad_scores, stripe_query, preferred_element_type=jnp.float32
    )
    value_total = jnp.einsum(
        "ghab,gahe->gbhe", probs_half, stripe_grad, preferred_element_type=jnp.float32
    )
    return (key_total * (1.0 / math.sqrt(HD)), value_total)


def in_blocks(step, carry, arrays, size):
    length = arrays[0].shape[0]

    def turn(index, total):
        parts = tuple((lax.dynamic_slice_in_dim(array, index * size, size, 0) for array in arrays))
        return step(total, parts)

    return lax.fori_loop(0, length // size, turn, carry)


def local_general(queries, key_map, value_map, saved_output, output_grad, saved_logsum):
    rows, cols, width = queries.shape
    half = HEADS // 2
    split = half * HD
    tail = (half, HD)
    block = 4 * rows
    products = output_grad.astype(jnp.float32) * saved_output.astype(jnp.float32)
    delta_all = jnp.sum(products.reshape(rows, cols, HEADS, HD), axis=3)

    def row_group(values, last):
        return values.reshape((rows // SW, SW * values.shape[1]) + last)

    def column_group(values, last):
        count = values.shape[0]
        shaped = values.reshape((count, cols // SW, SW) + last)
        return jnp.swapaxes(shaped, 0, 1).reshape((cols // SW, count * SW) + last)

    def column_back(values, count):
        shaped = values.reshape((cols // SW, count, SW, -1))
        return jnp.swapaxes(shaped, 0, 1).reshape(count, cols, -1)

    full_key, full_value = (
        lax.all_gather(key_map[:, :, :split], "col", axis=1, tiled=True),
        lax.all_gather(value_map[:, :, :split], "col", axis=1, tiled=True),
    )
    wide = full_key.shape[1]
    stripe_query = row_group(queries[:, :, :split], tail)
    stripe_grad = row_group(output_grad[:, :, :split], tail)
    stripe_logsum = row_group(saved_logsum[:, :, :half], (half,))
    stripe_delta = row_group(delta_all[:, :, :half], (half,))
    stripe_key = row_group(full_key, tail)
    stripe_value = row_group(full_value, tail)
    probs_half, grad_scores = attention_terms(
        stripe_query, stripe_key, stripe_value, stripe_grad, stripe_logsum, stripe_delta
    )
    row_query_grad = query_side(grad_scores, stripe_key).reshape(rows, cols, split)
    row_key_part, row_value_part = key_side(probs_half, grad_scores, stripe_query, stripe_grad)
    row_term = jnp.concatenate(
        (row_key_part.reshape(rows, wide, split), row_value_part.reshape(rows, wide, split)), axis=2
    )
    row_sums = lax.psum_scatter(row_term, "col", scatter_dimension=1, tiled=True)
    local_key = key_map[:, :, split:]
    local_value = value_map[:, :, split:]
    column_query = column_group(queries[:, :, split:], tail)
    column_grad = column_group(output_grad[:, :, split:], tail)
    column_logsum = column_group(saved_logsum[:, :, half:], (half,))
    column_delta = column_group(delta_all[:, :, half:], (half,))

    def query_step(total, pieces):
        grouped_key = column_group(pieces[0], tail)
        grouped_value = column_group(pieces[1], tail)
        weights, gradients = attention_terms(
            column_query, grouped_key, grouped_value, column_grad, column_logsum, column_delta
        )
        return total + query_side(gradients, grouped_key)

    empty_query = jnp.zeros(column_query.shape, jnp.float32)
    every_key, every_value = (
        lax.all_gather(local_key, "row", axis=0, tiled=True),
        lax.all_gather(local_value, "row", axis=0, tiled=True),
    )
    column_total = in_blocks(query_step, empty_query, (every_key, every_value), block)

    def key_step(pieces):
        count = pieces[0].shape[0]
        grouped_key = column_group(pieces[0], tail)
        grouped_value = column_group(pieces[1], tail)
        weights, gradients = attention_terms(
            column_query, grouped_key, grouped_value, column_grad, column_logsum, column_delta
        )
        key_part, value_part = key_side(weights, gradients, column_query, column_grad)
        return jnp.concatenate(
            (column_back(key_part, count), column_back(value_part, count)), axis=2
        )

    count = rows * lax.axis_size("row")
    stacked = lax.map(
        key_step,
        (
            every_key.reshape((count // block, block) + every_key.shape[1:]),
            every_value.reshape((count // block, block) + every_value.shape[1:]),
        ),
    )
    column_sums = lax.psum_scatter(
        stacked.reshape((count,) + stacked.shape[2:]), "row", scatter_dimension=0, tiled=True
    )
    column_key_grad = column_sums[:, :, :split]
    column_value_grad = column_sums[:, :, split:]
    column_query_grad = column_back(column_total, rows)
    query_grad = jnp.concatenate((row_query_grad, column_query_grad), axis=2)
    key_grad = jnp.concatenate((row_sums[:, :, :split], column_key_grad), axis=2)
    value_grad = jnp.concatenate((row_sums[:, :, split:], column_value_grad), axis=2)
    return (query_grad, key_grad, value_grad)


MESH = pl.DeviceIdType.MESH
NT = (((1,), (1,)), ((), ()))
TN = (((0,), (0,)), ((), ()))
PAIR = 2 * HD


def flat(values):
    return values.astype(jnp.float32).reshape((-1, values.shape[-1]))


def attend_part(count, block, j, q_s, k_s, v_s, g_s, rows, dq_t, dk_s, dv_s):
    scale = 1.0 / math.sqrt(HD)
    lane = lax.broadcasted_iota(jnp.int32, (block, PAIR), 1)
    masks = tuple(((lane // HD) == h).astype(jnp.float32).astype(jnp.bfloat16) for h in (0, 1))

    part = pl.ds(pl.multiple_of(j * block, block), block)
    q = q_s[0:count, :]
    g = g_s[0:count, :]
    keys = k_s[part, :]
    values = v_s[part, :]
    dk = []
    dv = []
    dq = None
    for h in (0, 1):
        key = keys * masks[h]
        value = values * masks[h]
        scores = lax.dot_general(key, q, NT, preferred_element_type=jnp.float32)
        probs = jnp.exp(scores * scale - rows[h : h + 1, 0:count])
        grad_probs = lax.dot_general(value, g, NT, preferred_element_type=jnp.float32)
        grad_scores = (probs * (grad_probs - rows[2 + h : 3 + h, 0:count])).astype(jnp.bfloat16)
        half = probs.astype(jnp.bfloat16)
        dv.append(jnp.dot(half, g, preferred_element_type=jnp.float32))
        dk.append(jnp.dot(grad_scores, q, preferred_element_type=jnp.float32))
        term = lax.dot_general(key, grad_scores, TN, preferred_element_type=jnp.float32)
        dq = term if dq is None else dq + term
    dk_s[part, :] = jnp.where(lane < HD, dk[0], dk[1]) * scale
    dv_s[part, :] = jnp.where(lane < HD, dv[0], dv[1])
    dq_t[:, 0:count] += dq


def exchange_kernel(
    q_hbm, k_hbm, v_hbm, o_hbm, g_hbm, l_hbm,
    dq_ref, dk_ref, dv_ref,
    col_in, col_aux, row_in, row_aux, aux_row, aux_col, col_out, row_out,
    q_s, k_s, v_s, g_s, rows_s, dq_t, dk_s, dv_s,
    q_ref, k_ref, v_ref, o_ref, g_ref, l_ref, row_own, keep_sem, in_sem,
    cs_sem, cr_sem, as_sem, ar_sem, rs_sem, rr_sem, os_sem, or_sem, ps_sem, pr_sem,
):
    me = lax.axis_index("row")
    core = lax.axis_index("col")
    peers = lax.axis_size("row")
    other = 1 - core
    split = (HEADS // 2) * HD
    pair = me // 2
    stripe = me % 2
    ins = (q_ref, k_ref, v_ref, g_ref)
    outs = (dq_ref, dk_ref, dv_ref)
    sources = (q_hbm, k_hbm, v_hbm, g_hbm)
    loads = [
        pltpu.make_async_copy(source, target, in_sem.at[n])
        for n, (source, target) in enumerate(
            (
                (g_hbm, g_ref), (o_hbm, o_ref), (l_hbm, l_ref),
                (q_hbm, q_ref), (k_hbm, k_ref), (v_hbm, v_ref),
            )
        )
    ]
    for load in loads:
        load.start()

    barrier = pltpu.get_barrier_semaphore()
    for step in range(1, peers):
        pl.semaphore_signal(
            barrier, inc=1, device_id={"row": lax.rem(me + step, peers)}, device_id_type=MESH
        )
    pl.semaphore_signal(barrier, inc=1, device_id={"col": other}, device_id_type=MESH)
    pl.semaphore_wait(barrier, peers)

    def col_lanes(index):
        return pl.ds(pl.multiple_of(split + PAIR * index, PAIR), PAIR)

    def core_lanes(index):
        return pl.ds(pl.multiple_of(2 * PAIR * index, 2 * PAIR), 2 * PAIR)

    def eight(index):
        return pl.ds(pl.multiple_of(index * 8, 8), 8)

    def row_copy(a):
        return pltpu.make_async_remote_copy(
            src_ref=sources[a].at[:, :, :, core_lanes(other)],
            dst_ref=row_in.at[a],
            send_sem=rs_sem.at[a], recv_sem=rr_sem.at[a],
            device_id={"col": other}, device_id_type=MESH,
        )

    def col_copy(a, target, source):
        return pltpu.make_async_remote_copy(
            src_ref=sources[a].at[:, target % 2, :, col_lanes(target // 2)],
            dst_ref=col_in.at[a, eight(source)],
            send_sem=cs_sem.at[a, target], recv_sem=cr_sem.at[a, source],
            device_id={"row": target}, device_id_type=MESH,
        )

    def aux_copy(target, source):
        return pltpu.make_async_remote_copy(
            src_ref=aux_col.at[target // 2],
            dst_ref=col_aux.at[source],
            send_sem=as_sem.at[target], recv_sem=ar_sem.at[source],
            device_id={"row": target}, device_id_type=MESH,
        )

    def back_copy(a, target, owner):
        return pltpu.make_async_remote_copy(
            src_ref=col_out.at[a, eight(target)],
            dst_ref=outs[a].at[:, owner % 2, :, col_lanes(owner // 2)],
            send_sem=os_sem.at[a, target], recv_sem=or_sem.at[a, owner],
            device_id={"row": target}, device_id_type=MESH,
        )

    def row_back(a, owner):
        return pltpu.make_async_remote_copy(
            src_ref=row_out.at[a],
            dst_ref=outs[a].at[:, :, :, core_lanes(owner)],
            send_sem=ps_sem.at[a], recv_sem=pr_sem.at[a],
            device_id={"col": other}, device_id_type=MESH,
        )

    def row_keep(a):
        return pltpu.make_async_copy(
            row_own.at[a], outs[a].at[:, :, :, core_lanes(core)], keep_sem.at[a]
        )

    def col_keep(a):
        return pltpu.make_async_copy(
            col_out.at[a, eight(me)], outs[a].at[:, stripe, :, col_lanes(pair)], keep_sem.at[3 + a]
        )

    def row_aux_copy():
        return pltpu.make_async_remote_copy(
            src_ref=aux_row.at[pl.ds(2 * other, 2)],
            dst_ref=row_aux,
            send_sem=rs_sem.at[4], recv_sem=rr_sem.at[4],
            device_id={"col": other}, device_id_type=MESH,
        )

    for a in range(4):
        row_copy(a).start()

    def partner(step):
        flip = jnp.where(step < 5, step + 3, step - 4)
        return (me // 4 + flip // 4) % 2 * 4 + (me // 2 + flip // 2) % 2 * 2 + (me + flip) % 2

    def send(step, carry):
        target = partner(step)
        for a in (0, 3):
            col_copy(a, target, me).start()
        return carry

    lax.fori_loop(1, peers, send, 0)

    for load in loads[:3]:
        load.wait()
    which = lax.broadcasted_iota(jnp.int32, (8, PAIR), 0)
    lane = lax.broadcasted_iota(jnp.int32, (8, PAIR), 1)
    pick = (which == 2 + lane // HD).astype(jnp.float32)
    which_l = lax.broadcasted_iota(jnp.int32, (8, HEADS), 0)
    lane_l = lax.broadcasted_iota(jnp.int32, (8, HEADS), 1)
    sums_row = flat(l_ref[...])
    sums_col = jnp.concatenate((flat(l_ref[:, 0]), flat(l_ref[:, 1])), axis=0)
    exact = functools.partial(
        lax.dot_general, dimension_numbers=NT, precision=lax.Precision.HIGHEST,
        preferred_element_type=jnp.float32,
    )
    for t in range(HEADS // 2):
        part = slice(t * PAIR, (t + 1) * PAIR)
        choose = ((lane_l - 2 * t == which_l) & (which_l < 2)).astype(jnp.float32)
        if t < HEADS // 4:
            products = flat(g_ref[:, :, :, part]) * flat(o_ref[:, :, :, part])
            aux_row[t] = exact(pick, products) + exact(choose, sums_row)
        else:
            products = jnp.concatenate(
                tuple(flat(g_ref[:, s, :, part]) * flat(o_ref[:, s, :, part]) for s in (0, 1)),
                axis=0,
            )
            aux_col[t - HEADS // 4] = exact(pick, products) + exact(choose, sums_col)

    row_aux_copy().start()

    def send_aux(step, carry):
        aux_copy(partner(step), me).start()
        return carry

    lax.fori_loop(1, peers, send_aux, 0)

    def send_keys(step, carry):
        target = partner(step)
        for a in (1, 2):
            col_copy(a, target, me).start()
        return carry

    lax.fori_loop(1, peers, send_keys, 0)
    for load in loads[3:]:
        load.wait()
    for a in range(4):
        col_in[a, eight(me)] = ins[a][:, stripe, :, col_lanes(pair)]
    col_aux[me] = aux_col[pair]

    for a in range(4):
        row_copy(a).wait_recv()
    row_aux_copy().wait_recv()
    scratch = (q_s, k_s, v_s, g_s)
    for u in (0, 1):
        part = slice(u * PAIR, (u + 1) * PAIR)
        mine = pl.ds(pl.multiple_of(2 * PAIR * core + u * PAIR, PAIR), PAIR)
        for a in range(4):
            scratch[a][0:128, :] = flat(ins[a][:, :, :, mine]).astype(jnp.bfloat16)
            scratch[a][128:256, :] = flat(row_in[a, :, :, :, part]).astype(jnp.bfloat16)
        rows_s[:, 0:128] = aux_row[2 * core + u]
        rows_s[:, 128:256] = row_aux[u]
        dq_t[:, 0:256] = jnp.zeros((PAIR, 256), jnp.float32)
        attend_part(256, 256, 0, q_s, k_s, v_s, g_s, rows_s, dq_t, dk_s, dv_s)
        dq = dq_t[:, 0:256].T * (1.0 / math.sqrt(HD))
        for a, grads in enumerate((dq, dk_s[0:256, :], dv_s[0:256, :])):
            shaped = grads.reshape((2, 8, 2, 8, PAIR)).astype(jnp.bfloat16)
            row_own[a, :, :, :, part] = shaped[0]
            row_out[a, :, :, :, part] = shaped[1]
    for a in range(3):
        row_back(a, core).start()
        row_keep(a).start()

    def arrive(step, carry):
        source = partner(step)
        for a in (0, 3):
            col_copy(a, source, source).wait_recv()
        aux_copy(source, source).wait_recv()
        return carry

    lax.fori_loop(1, peers, arrive, 0)
    for a in (0, 3):
        scratch[a][...] = flat(col_in[a]).astype(jnp.bfloat16)
    low = lane < HD
    for k in range(4):
        first = col_aux[2 * k]
        second = col_aux[2 * k + 1]
        even = jnp.where(low, first, pltpu.roll(second, HD, 1))
        odd = jnp.where(low, pltpu.roll(first, HD, 1), second)
        rows_s[:, k * PAIR : (k + 1) * PAIR] = jnp.where(stripe == 0, even, odd)
    dq_t[...] = jnp.zeros((PAIR, 512), jnp.float32)

    def chunk(two, others):
        for other_row in others:
            for a in (1, 2):
                col_copy(a, other_row, other_row).wait_recv()
        part = pl.ds(pl.multiple_of(two * PAIR, PAIR), PAIR)
        tiles = pl.ds(pl.multiple_of(two * 16, 16), 16)
        for a in (1, 2):
            scratch[a][part, :] = flat(col_in[a, tiles]).astype(jnp.bfloat16)
        attend_part(512, PAIR, two, q_s, k_s, v_s, g_s, rows_s, dq_t, dk_s, dv_s)
        for a, grads in ((1, dk_s), (2, dv_s)):
            col_out[a, tiles] = grads[part, :].reshape((16, 8, PAIR)).astype(jnp.bfloat16)
        for other_row in others:
            for a in (1, 2):
                back_copy(a, other_row, me).start()

    chunk(me // 2, (me + 1 - 2 * (me % 2),))

    def later(step, carry):
        two = (me // 4 + step // 2) % 2 * 2 + (me // 2 + step) % 2
        chunk(two, (2 * two, 2 * two + 1))
        return carry

    lax.fori_loop(1, peers // 2, later, 0)
    dq = dq_t[...].T * (1.0 / math.sqrt(HD))
    col_out[0] = dq.reshape((64, 8, PAIR)).astype(jnp.bfloat16)

    def give(step, carry):
        target = partner(step)
        back_copy(0, target, me).start()
        return carry

    lax.fori_loop(1, peers, give, 0)
    for a in range(3):
        col_keep(a).start()

    def finish(step, carry):
        target = partner(step)
        for a in range(3):
            back_copy(a, target, target).wait_recv()
        for a in range(3):
            back_copy(a, target, me).wait_send()
        for a in range(4):
            col_copy(a, target, me).wait_send()
        aux_copy(target, me).wait_send()
        return carry

    for a in range(4):
        row_copy(a).wait_send()
    row_aux_copy().wait_send()
    for a in range(3):
        row_back(a, core).wait()
        row_keep(a).wait()
        col_keep(a).wait()
    lax.fori_loop(1, peers, finish, 0)


def local_exchange(peers, queries, key_map, value_map, saved_output, output_grad, saved_logsum):
    rows, cols, width = queries.shape

    def view(values):
        return values.reshape((rows, cols // SW, SW, values.shape[-1]))

    half = jnp.bfloat16
    hbm = pl.BlockSpec(memory_space=pltpu.HBM)
    dma = pltpu.SemaphoreType.DMA
    grads = pl.pallas_call(
        exchange_kernel,
        out_shape=(pltpu.VMEM((rows, cols // SW, SW, width), half),) * 3,
        in_specs=[hbm] * 6,
        out_specs=(pl.BlockSpec(memory_space=pltpu.VMEM),) * 3,
        scratch_shapes=[
            pltpu.VMEM((4, 8 * peers, SW, PAIR), half),
            pltpu.VMEM((peers, 8, PAIR), jnp.float32),
            pltpu.VMEM((4, rows, cols // SW, SW, 2 * PAIR), half),
            pltpu.VMEM((2, 8, PAIR), jnp.float32),
            pltpu.VMEM((4, 8, PAIR), jnp.float32),
            pltpu.VMEM((4, 8, PAIR), jnp.float32),
            pltpu.VMEM((3, 8 * peers, SW, PAIR), half),
            pltpu.VMEM((3, rows, cols // SW, SW, 2 * PAIR), half),
            pltpu.VMEM((512, PAIR), half),
            pltpu.VMEM((512, PAIR), half),
            pltpu.VMEM((512, PAIR), half),
            pltpu.VMEM((512, PAIR), half),
            pltpu.VMEM((8, 512), jnp.float32),
            pltpu.VMEM((PAIR, 512), jnp.float32),
            pltpu.VMEM((512, PAIR), jnp.float32),
            pltpu.VMEM((512, PAIR), jnp.float32),
            *(pltpu.VMEM((rows, cols // SW, SW, width), half) for _ in range(5)),
            pltpu.VMEM((rows, cols // SW, SW, HEADS), jnp.float32),
            pltpu.VMEM((3, rows, cols // SW, SW, 2 * PAIR), half),
            dma((6,)),
            dma((6,)),
            dma((4, peers)), dma((4, peers)), dma((peers,)), dma((peers,)),
            dma((5,)), dma((5,)), dma((3, peers)), dma((3, peers)), dma((3,)), dma((3,)),
        ],
        compiler_params=pltpu.CompilerParams(
            collective_id=0, has_side_effects=True, vmem_limit_bytes=61 * 1024 * 1024
        ),
    )(
        view(queries), view(key_map), view(value_map), view(saved_output), view(output_grad),
        view(saved_logsum),
    )
    return tuple(values.astype(jnp.float32).reshape(rows, cols, width) for values in grads)


def local(mesh, *arrays):
    peers = mesh.shape["row"]
    if peers == 8 and mesh.shape["col"] == 2 and arrays[0].shape == (8, 16, HEADS * HD):
        return local_exchange(peers, *arrays)
    return local_general(*arrays)


def solution(mesh):
    in_specs = (
        P(("grp", "row"), "col", None),
        P(("grp", "row"), "col", None),
        P(("grp", "row"), "col", None),
        P(("grp", "row"), "col", None),
        P(("grp", "row"), "col", None),
        P(("grp", "row"), "col", None),
    )
    out_specs = (
        P(("grp", "row"), "col", None),
        P(("grp", "row"), "col", None),
        P(("grp", "row"), "col", None),
    )
    return jax.shard_map(functools.partial(local, mesh), mesh=mesh, in_specs=in_specs, out_specs=out_specs, check_vma=False)
```

```python
import functools
import math

import jax
import jax.numpy as jnp
from jax import lax
from jax.experimental import pallas as pl
from jax.experimental.pallas import tpu as pltpu
from jax.sharding import PartitionSpec as P

HEADS = 16
HD = 64
SW = 8


def attention_terms(
    stripe_query, stripe_key, stripe_value, stripe_grad, stripe_logsum, stripe_delta
):
    scale = 1.0 / math.sqrt(HD)
    scores = (
        jnp.einsum("gahe,gbhe->ghab", stripe_query, stripe_key, preferred_element_type=jnp.float32)
        * scale
    )
    probs = jnp.exp(scores - jnp.swapaxes(stripe_logsum, 1, 2)[..., None])
    grad_probs = jnp.einsum(
        "gahe,gbhe->ghab", stripe_grad, stripe_value, preferred_element_type=jnp.float32
    )
    grad_scores = (probs * (grad_probs - jnp.swapaxes(stripe_delta, 1, 2)[..., None])).astype(
        jnp.bfloat16
    )
    return (probs.astype(jnp.bfloat16), grad_scores)


def query_side(grad_scores, stripe_key):
    total = jnp.einsum(
        "ghab,gbhe->gahe", grad_scores, stripe_key, preferred_element_type=jnp.float32
    )
    return total * (1.0 / math.sqrt(HD))


def key_side(probs_half, grad_scores, stripe_query, stripe_grad):
    key_total = jnp.einsum(
        "ghab,gahe->gbhe", grad_scores, stripe_query, preferred_element_type=jnp.float32
    )
    value_total = jnp.einsum(
        "ghab,gahe->gbhe", probs_half, stripe_grad, preferred_element_type=jnp.float32
    )
    return (key_total * (1.0 / math.sqrt(HD)), value_total)


def in_blocks(step, carry, arrays, size):
    length = arrays[0].shape[0]

    def turn(index, total):
        parts = tuple((lax.dynamic_slice_in_dim(array, index * size, size, 0) for array in arrays))
        return step(total, parts)

    return lax.fori_loop(0, length // size, turn, carry)


def local_general(queries, key_map, value_map, saved_output, output_grad, saved_logsum):
    rows, cols, width = queries.shape
    half = HEADS // 2
    split = half * HD
    tail = (half, HD)
    block = 4 * rows
    products = output_grad.astype(jnp.float32) * saved_output.astype(jnp.float32)
    delta_all = jnp.sum(products.reshape(rows, cols, HEADS, HD), axis=3)

    def row_group(values, last):
        return values.reshape((rows // SW, SW * values.shape[1]) + last)

    def column_group(values, last):
        count = values.shape[0]
        shaped = values.reshape((count, cols // SW, SW) + last)
        return jnp.swapaxes(shaped, 0, 1).reshape((cols // SW, count * SW) + last)

    def column_back(values, count):
        shaped = values.reshape((cols // SW, count, SW, -1))
        return jnp.swapaxes(shaped, 0, 1).reshape(count, cols, -1)

    full_key, full_value = (
        lax.all_gather(key_map[:, :, :split], "col", axis=1, tiled=True),
        lax.all_gather(value_map[:, :, :split], "col", axis=1, tiled=True),
    )
    wide = full_key.shape[1]
    stripe_query = row_group(queries[:, :, :split], tail)
    stripe_grad = row_group(output_grad[:, :, :split], tail)
    stripe_logsum = row_group(saved_logsum[:, :, :half], (half,))
    stripe_delta = row_group(delta_all[:, :, :half], (half,))
    stripe_key = row_group(full_key, tail)
    stripe_value = row_group(full_value, tail)
    probs_half, grad_scores = attention_terms(
        stripe_query, stripe_key, stripe_value, stripe_grad, stripe_logsum, stripe_delta
    )
    row_query_grad = query_side(grad_scores, stripe_key).reshape(rows, cols, split)
    row_key_part, row_value_part = key_side(probs_half, grad_scores, stripe_query, stripe_grad)
    row_term = jnp.concatenate(
        (row_key_part.reshape(rows, wide, split), row_value_part.reshape(rows, wide, split)), axis=2
    )
    row_sums = lax.psum_scatter(row_term, "col", scatter_dimension=1, tiled=True)
    local_key = key_map[:, :, split:]
    local_value = value_map[:, :, split:]
    column_query = column_group(queries[:, :, split:], tail)
    column_grad = column_group(output_grad[:, :, split:], tail)
    column_logsum = column_group(saved_logsum[:, :, half:], (half,))
    column_delta = column_group(delta_all[:, :, half:], (half,))

    def query_step(total, pieces):
        grouped_key = column_group(pieces[0], tail)
        grouped_value = column_group(pieces[1], tail)
        weights, gradients = attention_terms(
            column_query, grouped_key, grouped_value, column_grad, column_logsum, column_delta
        )
        return total + query_side(gradients, grouped_key)

    empty_query = jnp.zeros(column_query.shape, jnp.float32)
    every_key, every_value = (
        lax.all_gather(local_key, "row", axis=0, tiled=True),
        lax.all_gather(local_value, "row", axis=0, tiled=True),
    )
    column_total = in_blocks(query_step, empty_query, (every_key, every_value), block)

    def key_step(pieces):
        count = pieces[0].shape[0]
        grouped_key = column_group(pieces[0], tail)
        grouped_value = column_group(pieces[1], tail)
        weights, gradients = attention_terms(
            column_query, grouped_key, grouped_value, column_grad, column_logsum, column_delta
        )
        key_part, value_part = key_side(weights, gradients, column_query, column_grad)
        return jnp.concatenate(
            (column_back(key_part, count), column_back(value_part, count)), axis=2
        )

    count = rows * lax.axis_size("row")
    stacked = lax.map(
        key_step,
        (
            every_key.reshape((count // block, block) + every_key.shape[1:]),
            every_value.reshape((count // block, block) + every_value.shape[1:]),
        ),
    )
    column_sums = lax.psum_scatter(
        stacked.reshape((count,) + stacked.shape[2:]), "row", scatter_dimension=0, tiled=True
    )
    column_key_grad = column_sums[:, :, :split]
    column_value_grad = column_sums[:, :, split:]
    column_query_grad = column_back(column_total, rows)
    query_grad = jnp.concatenate((row_query_grad, column_query_grad), axis=2)
    key_grad = jnp.concatenate((row_sums[:, :, :split], column_key_grad), axis=2)
    value_grad = jnp.concatenate((row_sums[:, :, split:], column_value_grad), axis=2)
    return (query_grad, key_grad, value_grad)


MESH = pl.DeviceIdType.MESH
NT = (((1,), (1,)), ((), ()))
TN = (((0,), (0,)), ((), ()))
PAIR = 2 * HD


def flat(values):
    return values.astype(jnp.float32).reshape((-1, values.shape[-1]))


def attend_part(count, block, j, q_s, k_s, v_s, g_s, rows, dq_t, dk_s, dv_s):
    scale = 1.0 / math.sqrt(HD)
    lane = lax.broadcasted_iota(jnp.int32, (block, PAIR), 1)
    masks = tuple(((lane // HD) == h).astype(jnp.float32).astype(jnp.bfloat16) for h in (0, 1))

    part = pl.ds(pl.multiple_of(j * block, block), block)
    q = q_s[0:count, :]
    g = g_s[0:count, :]
    keys = k_s[part, :]
    values = v_s[part, :]
    dk = []
    dv = []
    dq = None
    for h in (0, 1):
        key = keys * masks[h]
        value = values * masks[h]
        scores = lax.dot_general(key, q, NT, preferred_element_type=jnp.float32)
        probs = jnp.exp(scores * scale - rows[h : h + 1, 0:count])
        grad_probs = lax.dot_general(value, g, NT, preferred_element_type=jnp.float32)
        grad_scores = (probs * (grad_probs - rows[2 + h : 3 + h, 0:count])).astype(jnp.bfloat16)
        half = probs.astype(jnp.bfloat16)
        dv.append(jnp.dot(half, g, preferred_element_type=jnp.float32))
        dk.append(jnp.dot(grad_scores, q, preferred_element_type=jnp.float32))
        term = lax.dot_general(key, grad_scores, TN, preferred_element_type=jnp.float32)
        dq = term if dq is None else dq + term
    dk_s[part, :] = jnp.where(lane < HD, dk[0], dk[1]) * scale
    dv_s[part, :] = jnp.where(lane < HD, dv[0], dv[1])
    dq_t[:, 0:count] += dq


def exchange_kernel(
    q_hbm, k_hbm, v_hbm, o_hbm, g_hbm, l_hbm,
    dq_ref, dk_ref, dv_ref,
    col_in, col_aux, row_in, row_aux, aux_row, aux_col, col_out, row_out,
    q_s, k_s, v_s, g_s, rows_s, dq_t, dk_s, dv_s,
    q_ref, k_ref, v_ref, o_ref, g_ref, l_ref, row_own, keep_sem, in_sem,
    cs_sem, cr_sem, as_sem, ar_sem, rs_sem, rr_sem, os_sem, or_sem, ps_sem, pr_sem,
):
    me = lax.axis_index("row")
    core = lax.axis_index("col")
    peers = lax.axis_size("row")
    other = 1 - core
    split = (HEADS // 2) * HD
    pair = me // 2
    stripe = me % 2
    ins = (q_ref, k_ref, v_ref, g_ref)
    outs = (dq_ref, dk_ref, dv_ref)
    sources = (q_hbm, k_hbm, v_hbm, g_hbm)
    loads = [
        pltpu.make_async_copy(source, target, in_sem.at[n])
        for n, (source, target) in enumerate(
            (
                (g_hbm, g_ref), (o_hbm, o_ref), (l_hbm, l_ref),
                (q_hbm, q_ref), (k_hbm, k_ref), (v_hbm, v_ref),
            )
        )
    ]
    for load in loads:
        load.start()

    barrier = pltpu.get_barrier_semaphore()
    for step in range(1, peers):
        pl.semaphore_signal(
            barrier, inc=1, device_id={"row": lax.rem(me + step, peers)}, device_id_type=MESH
        )
    pl.semaphore_signal(barrier, inc=1, device_id={"col": other}, device_id_type=MESH)
    pl.semaphore_wait(barrier, peers)

    def col_lanes(index):
        return pl.ds(pl.multiple_of(split + PAIR * index, PAIR), PAIR)

    def core_lanes(index):
        return pl.ds(pl.multiple_of(2 * PAIR * index, 2 * PAIR), 2 * PAIR)

    def eight(index):
        return pl.ds(pl.multiple_of(index * 8, 8), 8)

    def row_copy(a):
        return pltpu.make_async_remote_copy(
            src_ref=sources[a].at[:, :, :, core_lanes(other)],
            dst_ref=row_in.at[a],
            send_sem=rs_sem.at[a], recv_sem=rr_sem.at[a],
            device_id={"col": other}, device_id_type=MESH,
        )

    def col_copy(a, target, source):
        return pltpu.make_async_remote_copy(
            src_ref=sources[a].at[:, target % 2, :, col_lanes(target // 2)],
            dst_ref=col_in.at[a, eight(source)],
            send_sem=cs_sem.at[a, target], recv_sem=cr_sem.at[a, source],
            device_id={"row": target}, device_id_type=MESH,
        )

    def aux_copy(target, source):
        return pltpu.make_async_remote_copy(
            src_ref=aux_col.at[target // 2],
            dst_ref=col_aux.at[source],
            send_sem=as_sem.at[target], recv_sem=ar_sem.at[source],
            device_id={"row": target}, device_id_type=MESH,
        )

    def back_copy(a, target, owner):
        return pltpu.make_async_remote_copy(
            src_ref=col_out.at[a, eight(target)],
            dst_ref=outs[a].at[:, owner % 2, :, col_lanes(owner // 2)],
            send_sem=os_sem.at[a, target], recv_sem=or_sem.at[a, owner],
            device_id={"row": target}, device_id_type=MESH,
        )

    def row_back(a, owner):
        return pltpu.make_async_remote_copy(
            src_ref=row_out.at[a],
            dst_ref=outs[a].at[:, :, :, core_lanes(owner)],
            send_sem=ps_sem.at[a], recv_sem=pr_sem.at[a],
            device_id={"col": other}, device_id_type=MESH,
        )

    def row_keep(a):
        return pltpu.make_async_copy(
            row_own.at[a], outs[a].at[:, :, :, core_lanes(core)], keep_sem.at[a]
        )

    def col_keep(a):
        return pltpu.make_async_copy(
            col_out.at[a, eight(me)], outs[a].at[:, stripe, :, col_lanes(pair)], keep_sem.at[3 + a]
        )

    def row_aux_copy():
        return pltpu.make_async_remote_copy(
            src_ref=aux_row.at[pl.ds(2 * other, 2)],
            dst_ref=row_aux,
            send_sem=rs_sem.at[4], recv_sem=rr_sem.at[4],
            device_id={"col": other}, device_id_type=MESH,
        )

    for a in range(4):
        row_copy(a).start()

    def partner(step):
        flip = jnp.where(step < 5, step + 3, step - 4)
        return (me // 4 + flip // 4) % 2 * 4 + (me // 2 + flip // 2) % 2 * 2 + (me + flip) % 2

    def send(step, carry):
        target = partner(step)
        for a in (0, 3):
            col_copy(a, target, me).start()
        return carry

    lax.fori_loop(1, peers, send, 0)

    for load in loads[:3]:
        load.wait()
    which = lax.broadcasted_iota(jnp.int32, (8, PAIR), 0)
    lane = lax.broadcasted_iota(jnp.int32, (8, PAIR), 1)
    pick = (which == 2 + lane // HD).astype(jnp.float32)
    which_l = lax.broadcasted_iota(jnp.int32, (8, HEADS), 0)
    lane_l = lax.broadcasted_iota(jnp.int32, (8, HEADS), 1)
    sums_row = flat(l_ref[...])
    sums_col = jnp.concatenate((flat(l_ref[:, 0]), flat(l_ref[:, 1])), axis=0)
    exact = functools.partial(
        lax.dot_general, dimension_numbers=NT, precision=lax.Precision.HIGHEST,
        preferred_element_type=jnp.float32,
    )
    for t in range(HEADS // 2):
        part = slice(t * PAIR, (t + 1) * PAIR)
        choose = ((lane_l - 2 * t == which_l) & (which_l < 2)).astype(jnp.float32)
        if t < HEADS // 4:
            products = flat(g_ref[:, :, :, part]) * flat(o_ref[:, :, :, part])
            aux_row[t] = exact(pick, products) + exact(choose, sums_row)
        else:
            products = jnp.concatenate(
                tuple(flat(g_ref[:, s, :, part]) * flat(o_ref[:, s, :, part]) for s in (0, 1)),
                axis=0,
            )
            aux_col[t - HEADS // 4] = exact(pick, products) + exact(choose, sums_col)

    row_aux_copy().start()

    def send_aux(step, carry):
        aux_copy(partner(step), me).start()
        return carry

    lax.fori_loop(1, peers, send_aux, 0)

    def send_keys(step, carry):
        target = partner(peers - step)
        for a in (1, 2):
            col_copy(a, target, me).start()
        return carry

    lax.fori_loop(1, peers, send_keys, 0)
    for load in loads[3:]:
        load.wait()
    for a in range(4):
        col_in[a, eight(me)] = ins[a][:, stripe, :, col_lanes(pair)]
    col_aux[me] = aux_col[pair]

    for a in range(4):
        row_copy(a).wait_recv()
    row_aux_copy().wait_recv()
    scratch = (q_s, k_s, v_s, g_s)
    for u in (0, 1):
        part = slice(u * PAIR, (u + 1) * PAIR)
        mine = pl.ds(pl.multiple_of(2 * PAIR * core + u * PAIR, PAIR), PAIR)
        for a in range(4):
            scratch[a][0:128, :] = flat(ins[a][:, :, :, mine]).astype(jnp.bfloat16)
            scratch[a][128:256, :] = flat(row_in[a, :, :, :, part]).astype(jnp.bfloat16)
        rows_s[:, 0:128] = aux_row[2 * core + u]
        rows_s[:, 128:256] = row_aux[u]
        dq_t[:, 0:256] = jnp.zeros((PAIR, 256), jnp.float32)
        attend_part(256, 256, 0, q_s, k_s, v_s, g_s, rows_s, dq_t, dk_s, dv_s)
        dq = dq_t[:, 0:256].T * (1.0 / math.sqrt(HD))
        for a, grads in enumerate((dq, dk_s[0:256, :], dv_s[0:256, :])):
            shaped = grads.reshape((2, 8, 2, 8, PAIR)).astype(jnp.bfloat16)
            row_own[a, :, :, :, part] = shaped[0]
            row_out[a, :, :, :, part] = shaped[1]
    for a in range(3):
        row_back(a, core).start()
        row_keep(a).start()

    def arrive(step, carry):
        source = partner(step)
        for a in (0, 3):
            col_copy(a, source, source).wait_recv()
        aux_copy(source, source).wait_recv()
        return carry

    lax.fori_loop(1, peers, arrive, 0)
    for a in (0, 3):
        scratch[a][...] = flat(col_in[a]).astype(jnp.bfloat16)
    low = lane < HD
    for k in range(4):
        first = col_aux[2 * k]
        second = col_aux[2 * k + 1]
        even = jnp.where(low, first, pltpu.roll(second, HD, 1))
        odd = jnp.where(low, pltpu.roll(first, HD, 1), second)
        rows_s[:, k * PAIR : (k + 1) * PAIR] = jnp.where(stripe == 0, even, odd)
    dq_t[...] = jnp.zeros((PAIR, 512), jnp.float32)

    def chunk(two, others):
        for other_row in others:
            for a in (1, 2):
                col_copy(a, other_row, other_row).wait_recv()
        part = pl.ds(pl.multiple_of(two * PAIR, PAIR), PAIR)
        tiles = pl.ds(pl.multiple_of(two * 16, 16), 16)
        for a in (1, 2):
            scratch[a][part, :] = flat(col_in[a, tiles]).astype(jnp.bfloat16)
        attend_part(512, PAIR, two, q_s, k_s, v_s, g_s, rows_s, dq_t, dk_s, dv_s)
        for a, grads in ((1, dk_s), (2, dv_s)):
            col_out[a, tiles] = grads[part, :].reshape((16, 8, PAIR)).astype(jnp.bfloat16)
        for other_row in others:
            for a in (1, 2):
                back_copy(a, other_row, me).start()

    chunk(me // 2, (me + 1 - 2 * (me % 2),))

    def later(step, carry):
        two = (me // 4 + step // 2) % 2 * 2 + (me // 2 + step) % 2
        chunk(two, (2 * two, 2 * two + 1))
        return carry

    lax.fori_loop(1, peers // 2, later, 0)
    dq = dq_t[...].T * (1.0 / math.sqrt(HD))
    col_out[0] = dq.reshape((64, 8, PAIR)).astype(jnp.bfloat16)

    def give(step, carry):
        target = partner(step)
        back_copy(0, target, me).start()
        return carry

    lax.fori_loop(1, peers, give, 0)
    for a in range(3):
        col_keep(a).start()

    def finish(step, carry):
        target = partner(step)
        for a in range(3):
            back_copy(a, target, target).wait_recv()
        for a in range(3):
            back_copy(a, target, me).wait_send()
        for a in range(4):
            col_copy(a, target, me).wait_send()
        aux_copy(target, me).wait_send()
        return carry

    for a in range(4):
        row_copy(a).wait_send()
    row_aux_copy().wait_send()
    for a in range(3):
        row_back(a, core).wait()
        row_keep(a).wait()
        col_keep(a).wait()
    lax.fori_loop(1, peers, finish, 0)


def local_exchange(peers, queries, key_map, value_map, saved_output, output_grad, saved_logsum):
    rows, cols, width = queries.shape

    def view(values):
        return values.reshape((rows, cols // SW, SW, values.shape[-1]))

    half = jnp.bfloat16
    hbm = pl.BlockSpec(memory_space=pltpu.HBM)
    dma = pltpu.SemaphoreType.DMA
    grads = pl.pallas_call(
        exchange_kernel,
        out_shape=(pltpu.VMEM((rows, cols // SW, SW, width), half),) * 3,
        in_specs=[hbm] * 6,
        out_specs=(pl.BlockSpec(memory_space=pltpu.VMEM),) * 3,
        scratch_shapes=[
            pltpu.VMEM((4, 8 * peers, SW, PAIR), half),
            pltpu.VMEM((peers, 8, PAIR), jnp.float32),
            pltpu.VMEM((4, rows, cols // SW, SW, 2 * PAIR), half),
            pltpu.VMEM((2, 8, PAIR), jnp.float32),
            pltpu.VMEM((4, 8, PAIR), jnp.float32),
            pltpu.VMEM((4, 8, PAIR), jnp.float32),
            pltpu.VMEM((3, 8 * peers, SW, PAIR), half),
            pltpu.VMEM((3, rows, cols // SW, SW, 2 * PAIR), half),
            pltpu.VMEM((512, PAIR), half),
            pltpu.VMEM((512, PAIR), half),
            pltpu.VMEM((512, PAIR), half),
            pltpu.VMEM((512, PAIR), half),
            pltpu.VMEM((8, 512), jnp.float32),
            pltpu.VMEM((PAIR, 512), jnp.float32),
            pltpu.VMEM((512, PAIR), jnp.float32),
            pltpu.VMEM((512, PAIR), jnp.float32),
            *(pltpu.VMEM((rows, cols // SW, SW, width), half) for _ in range(5)),
            pltpu.VMEM((rows, cols // SW, SW, HEADS), jnp.float32),
            pltpu.VMEM((3, rows, cols // SW, SW, 2 * PAIR), half),
            dma((6,)),
            dma((6,)),
            dma((4, peers)), dma((4, peers)), dma((peers,)), dma((peers,)),
            dma((5,)), dma((5,)), dma((3, peers)), dma((3, peers)), dma((3,)), dma((3,)),
        ],
        compiler_params=pltpu.CompilerParams(
            collective_id=0, has_side_effects=True, vmem_limit_bytes=61 * 1024 * 1024
        ),
    )(
        view(queries), view(key_map), view(value_map), view(saved_output), view(output_grad),
        view(saved_logsum),
    )
    return tuple(values.astype(jnp.float32).reshape(rows, cols, width) for values in grads)


def local(mesh, *arrays):
    peers = mesh.shape["row"]
    if peers == 8 and mesh.shape["col"] == 2 and arrays[0].shape == (8, 16, HEADS * HD):
        return local_exchange(peers, *arrays)
    return local_general(*arrays)


def solution(mesh):
    in_specs = (
        P(("grp", "row"), "col", None),
        P(("grp", "row"), "col", None),
        P(("grp", "row"), "col", None),
        P(("grp", "row"), "col", None),
        P(("grp", "row"), "col", None),
        P(("grp", "row"), "col", None),
    )
    out_specs = (
        P(("grp", "row"), "col", None),
        P(("grp", "row"), "col", None),
        P(("grp", "row"), "col", None),
    )
    return jax.shard_map(functools.partial(local, mesh), mesh=mesh, in_specs=in_specs, out_specs=out_specs, check_vma=False)
```
